256 devices in a mesh: space: 32 (over z_lo, y, core), snap: 8 (over z_hi, x).
Axes of the slice: x: 4, y: 4, z: 8 (z_hi: 2, z_lo: 4; z = z_hi * 4 + z_lo), core: 2. Of those that a mesh axis runs over, the one named last changes fastest.
Arguments:
- forcing_direct: bfloat16 [1024, 32, 16, 128], P('snap', 'space'), may hold values from -6 to 6
- forcing_adjoint: bfloat16 [1024, 32, 16, 128], P('snap', 'space'), may hold values from -6 to 6
- conductance: float32 [32, 16, 128], P('space'), may hold values from 0.25 to 4
- shift_table: float32 [16], replicated, may hold values from 0.2 to 3
- freq_direct: int32 [1024], P('snap'), may hold values from 0 to 15
- freq_adjoint: int32 [1024], P('snap'), may hold values from 0 to 15
- left_factors: float32 [1024, 64], replicated, may hold values from -0.1875 to 0.1875
- right_factors: float32 [1024, 64], replicated, may hold values from -0.1875 to 0.1875
- singular_values: float32 [64], replicated, may hold values from 0.25 to 4
Outputs:
- gram: float32 [1024, 1024], P('snap', 'space')
- direct_modes: float32 [64, 32, 16, 128], P(None, 'space', 'snap')
- adjoint_modes: float32 [64, 32, 16, 128], P(None, 'space', 'snap')
The draws below stay inside these ranges and needn't reach their ends.
All inputs are finite; a program needn't handle non-finite values.
Results may differ from the reference program's by a relative error of at most 0.0041.
Values may be sent and summed in bfloat16 or wider, within the bound.
A program may use at most 64 MiB of HBM per device.

```python
import math
import jax
import jax.numpy as jnp
from jax import lax

NS = 1024
R = 64
NF = 16
GY = 16
GZ = 128
NX = 32


def set_ends(values, stream_key, least, largest):
    dims = values.shape
    spot = [jax.random.randint(jax.random.fold_in(stream_key, axis), (), 0, dims[axis]) for axis in range(len(dims))]
    values = values.at[tuple(spot)].set(least)
    longest = dims.index(max(dims))
    spot[longest] = (spot[longest] + 1) % dims[longest]
    return values.at[tuple(spot)].set(largest)


def level_of(own_key, dims, cuts, low, high):
    gain = 1.0
    for position, parts in cuts:
        steps = jax.random.uniform(jax.random.fold_in(jax.random.fold_in(own_key, 6), position), (parts,), jnp.float32, low / len(cuts), high / len(cuts))
        gain = gain * jnp.repeat(jnp.exp(steps), dims[position] // parts).reshape((-1,) + (1,) * (len(dims) - 1 - position))
    return gain


def noise(own_key, dims, width, reach, cuts=(), kind=jnp.bfloat16):
    entries = jax.random.normal(own_key, dims, jnp.float32) * width
    if len(cuts) > 0:
        entries = level_of(own_key, dims, cuts, -0.22, 0.18) * entries
    return jnp.clip(entries, min=-reach, max=reach).astype(kind)


def setup_inputs(seed: int = 0) -> dict:
    arg_keys = jax.random.split(jax.random.key(seed), 10)
    return {
        "forcing_direct": noise(arg_keys[0], (NS, NX, GY, GZ), 1.0, 6.0, ((0, 8), (1, 32))),
        "forcing_adjoint": noise(arg_keys[1], (NS, NX, GY, GZ), 1.0, 6.0, ((0, 8), (1, 32))),
        "conductance": jnp.clip(jnp.exp(math.log(4.0) - 2.7725887 * jax.random.uniform(arg_keys[2], (NX, GY, GZ), jnp.float32) ** level_of(arg_keys[2], (NX, GY, GZ), ((0, 32),), -0.2, 0.2)), 0.25, 4.0),
        "shift_table": jnp.clip(jnp.exp(jax.random.uniform(arg_keys[3], (NF,), jnp.float32, math.log(0.2), math.log(3.0))), 0.2, 3.0),
        "freq_direct": set_ends(jax.random.randint(arg_keys[4], (NS,), 0, NF), jax.random.fold_in(arg_keys[4], 1), 0, NF - 1).astype(jnp.int32),
        "freq_adjoint": set_ends(jax.random.randint(arg_keys[5], (NS,), 0, NF), jax.random.fold_in(arg_keys[5], 1), 0, NF - 1).astype(jnp.int32),
        "left_factors": noise(arg_keys[6], (NS, R), NS ** -0.5, 0.1875, (), jnp.float32),
        "right_factors": noise(arg_keys[7], (NS, R), NS ** -0.5, 0.1875, (), jnp.float32),
        "singular_values": jnp.clip(jnp.exp(jax.random.uniform(arg_keys[8], (R,), jnp.float32, math.log(0.25), math.log(4.0))), 0.25, 4.0),
    }


def lookup(indices, shift_list):
    levels = jnp.arange(shift_list.shape[0], dtype=jnp.int32)
    picked = jnp.where(indices[:, None] == levels[None, :], shift_list[None, :], jnp.float32(0.0))
    return lax.optimization_barrier(jnp.sum(picked, axis=1))

def neighbours(values):
    padded = jnp.pad(values, ((0, 0), (1, 1), (1, 1), (1, 1)))
    summed = padded[:, 2:, 1:-1, 1:-1] + padded[:, :-2, 1:-1, 1:-1]
    summed = summed + padded[:, 1:-1, 2:, 1:-1] + padded[:, 1:-1, :-2, 1:-1]
    return summed + padded[:, 1:-1, 1:-1, 2:] + padded[:, 1:-1, 1:-1, :-2]

def sweeps(direct_force, adjoint_force, direct_shift, adjoint_shift, conductance):
    coeff = conductance[None]
    direct_diag = direct_shift[:, None, None, None] + 6.0 * coeff
    adjoint_diag = adjoint_shift[:, None, None, None] + 6.0 * coeff
    force_dir = direct_force.astype(jnp.float32)
    force_adj = adjoint_force.astype(jnp.float32)
    state_dir = force_dir / direct_diag
    state_adj = force_adj / adjoint_diag
    for repeat in range(2):
        state_dir = (force_dir + coeff * neighbours(state_dir)) / direct_diag
        state_adj = (force_adj + neighbours(coeff * state_adj)) / adjoint_diag
    return (state_dir.astype(jnp.bfloat16), state_adj.astype(jnp.bfloat16))

def reference(forcing_direct, forcing_adjoint, conductance, shift_table, freq_direct, freq_adjoint, left_factors, right_factors, singular_values):
    block_rows = math.gcd(NS, 128)
    blocks_count = NS // block_rows
    shift_dir = lookup(freq_direct, shift_table)
    shift_adj = lookup(freq_adjoint, shift_table)

    def one_block(pieces):
        return sweeps(pieces[0], pieces[1], pieces[2], pieces[3], conductance)
    direct, adjoint = lax.map(one_block, (forcing_direct.reshape(blocks_count, block_rows, NX, GY, GZ), forcing_adjoint.reshape(blocks_count, block_rows, NX, GY, GZ), shift_dir.reshape(blocks_count, block_rows), shift_adj.reshape(blocks_count, block_rows)))
    direct = direct.reshape(NS, NX * GY * GZ)
    adjoint = adjoint.reshape(NS, NX * GY * GZ)
    weight = 1.0 / math.sqrt(NX * GY * GZ)
    gram = jnp.dot(adjoint, direct.T, preferred_element_type=jnp.float32) * weight
    inv_root = 1.0 / jnp.sqrt(singular_values)
    right_scaled = (right_factors * inv_root[None, :]).astype(jnp.bfloat16)
    left_scaled = (left_factors * inv_root[None, :]).astype(jnp.bfloat16)
    direct_modes = jnp.dot(right_scaled.T, direct, preferred_element_type=jnp.float32).reshape(R, NX, GY, GZ)
    adjoint_modes = jnp.dot(left_scaled.T, adjoint, preferred_element_type=jnp.float32).reshape(R, NX, GY, GZ)
    return (gram, direct_modes, adjoint_modes)
```

```python
import functools
import math

import jax
import jax.numpy as jnp
from jax import lax
from jax.experimental import pallas as pl
from jax.experimental.pallas import tpu as pltpu
from jax.sharding import PartitionSpec as P

MESH = pl.DeviceIdType.MESH
F32 = jnp.float32
BF16 = jnp.bfloat16

ROWS = 16
LANES = 128
PLANES = 6
PART = 32
LEVELS = 16


def contract_last(a, b):
    return lax.dot_general(a, b, (((1,), (1,)), ((), ())), preferred_element_type=F32)


def contract_first(a, b):
    return lax.dot_general(a, b, (((0,), (0,)), ((), ())), preferred_element_type=F32)


def kernel(
    weight,
    fd, fa, cond, table, freq_d, freq_a, left, right, sing,
    gram_o, dm_o, am_o,
    field, chalo, rtab, crtab, turn, outbox, dirbox, adjbox,
    psend, precv, gsum, bsend, brecv, mpart, mrecv, lbuf, rbuf,
    halo_s, halo_r, cond_s, cond_r, load_s, post_s, post_r, sa_s, sa_r, sb_s, sb_r, md_s, md_r,
):
    s = lax.axis_index("space")
    p = lax.axis_index("snap")
    j, h = s // 2, s % 2
    zl, y = j // 4, j % 4
    zh, x = p // 4, p % 4
    forcing = (fd, fa)

    def dev(ss, pp):
        return (ss, pp)

    barrier = pltpu.get_barrier_semaphore()
    greet = [dev(2 * j + 1 - h, p)]
    for dj in (-1, 1):
        for dh in (0, 1):
            greet.append(dev(2 * ((j + dj + 16) % 16) + dh, p))
    for dz in range(2):
        for dx in range(4):
            if dz or dx:
                greet.append(dev(s, ((zh + dz) % 2) * 4 + (x + dx) % 4))
    for dx in range(1, 4):
        greet.append(dev(2 * j + 1 - h, zh * 4 + (x + dx) % 4))
    for dy in range(1, 4):
        for dx in range(4):
            greet.append(dev(2 * (zl * 4 + (y + dy) % 4) + h, zh * 4 + (x + dx) % 4))
    for dz in range(1, 4):
        greet.append(dev(2 * (((zl + dz) % 4) * 4 + y) + h, p))
    for target in greet:
        pl.semaphore_signal(barrier, inc=1, device_id=target, device_id_type=MESH)
    pl.semaphore_wait(barrier, len(greet))

    def start_row(fam, part, half):
        return part * 64 + half * 32 if fam == 0 else half * 64 + part * 32

    def halo_copy(c, dj, half):
        fam, part = c // 2, c % 2
        slot = 2 * (dj + 1)
        return pltpu.make_async_remote_copy(
            src_ref=forcing[fam].at[pl.ds(start_row(fam, part, half), PART)],
            dst_ref=field.at[fam, part, 2 * (1 - dj) + h],
            send_sem=halo_s.at[c, slot + half],
            recv_sem=halo_r.at[c, 2 * (1 - dj) + h],
            device_id=dev(2 * (j + dj) + half, p),
            device_id_type=MESH,
        )

    def halo_own(c):
        fam, part = c // 2, c % 2
        return pltpu.make_async_copy(
            forcing[fam].at[pl.ds(start_row(fam, part, h), PART)],
            field.at[fam, part, 2 + h],
            load_s.at[c],
        )

    def cond_copy(dj, half):
        return pltpu.make_async_remote_copy(
            src_ref=cond,
            dst_ref=chalo.at[2 * (1 - dj) + h],
            send_sem=cond_s.at[2 * (dj + 1) + half],
            recv_sem=cond_r.at[2 * (1 - dj) + h],
            device_id=dev(2 * (j + dj) + half, p),
            device_id_type=MESH,
        )

    def to_neighbours(act):
        for dj, inside in ((1, j < 15), (-1, j > 0)):
            @pl.when(inside)
            def _():
                for half in range(2):
                    act(dj, half)
        act(0, 1 - h)

    def from_neighbours(act):
        for dj, inside in ((-1, j > 0), (1, j < 15)):
            @pl.when(inside)
            def _():
                for half in range(2):
                    act(dj, half)
        act(0, 1 - h)

    to_neighbours(lambda dj, half: cond_copy(dj, half).start())
    for c in range(4):
        to_neighbours(lambda dj, half: halo_copy(c, dj, half).start())
        halo_own(c).start()
    lcopy = pltpu.make_async_copy(left.at[pl.ds(zh * 4, 4)], lbuf, load_s.at[4])
    rcopy = pltpu.make_async_copy(right.at[:, :, h], rbuf, load_s.at[5])
    ccopy = pltpu.make_async_copy(cond, chalo.at[2 + h], load_s.at[6])
    lcopy.start()
    rcopy.start()
    ccopy.start()

    for first, edge in ((0, j == 0), (4, j == 15)):
        @pl.when(edge)
        def _():
            for k in range(2):
                chalo[first + k] = jnp.ones((ROWS, LANES), F32)
                for fam in range(2):
                    for part in range(2):
                        field[fam, part, first + k] = jnp.zeros((PART, ROWS, LANES), BF16)

    def cond_arrival(dj, half):
        pltpu.make_async_remote_copy(
            src_ref=cond,
            dst_ref=chalo.at[2 * (1 + dj) + half],
            send_sem=cond_s.at[0],
            recv_sem=cond_r.at[2 * (1 + dj) + half],
            device_id=dev(s, p),
            device_id_type=MESH,
        ).wait_recv()

    def halo_arrival(c):
        fam, part = c // 2, c % 2

        def act(dj, half):
            pltpu.make_async_remote_copy(
                src_ref=forcing[fam].at[pl.ds(0, PART)],
                dst_ref=field.at[fam, part, 2 * (1 + dj) + half],
                send_sem=halo_s.at[c, 0],
                recv_sem=halo_r.at[c, 2 * (1 + dj) + half],
                device_id=dev(s, p),
                device_id_type=MESH,
            ).wait_recv()

        return act

    ccopy.wait()
    from_neighbours(cond_arrival)

    def fill(level, carry):
        shift = table[level]
        for q in range(PLANES):
            there = j + (q // 2 - 1)
            mask = jnp.where((there >= 0) & (there < 16), F32(1.0), F32(0.0))
            coeff = chalo[q]
            inverse = mask / (shift + 6.0 * coeff)
            rtab[level, q] = inverse
            crtab[level, q] = coeff * inverse
        return carry

    lax.fori_loop(0, LEVELS, fill, 0)

    row = lax.broadcasted_iota(jnp.int32, (ROWS, LANES), 0)
    lane = lax.broadcasted_iota(jnp.int32, (ROWS, LANES), 1)

    def flat_sum(v):
        up = jnp.where(row == 0, 0.0, pltpu.roll(v, 1, 0))
        down = jnp.where(row == ROWS - 1, 0.0, pltpu.roll(v, ROWS - 1, 0))
        fore = jnp.where(lane == 0, 0.0, pltpu.roll(v, 1, 1))
        aft = jnp.where(lane == LANES - 1, 0.0, pltpu.roll(v, LANES - 1, 1))
        return (up + down) + (fore + aft)

    def smooth(fam, part):
        freq = freq_d if fam == 0 else freq_a
        base = start_row(fam, part, h)

        def one(n, carry):
            level = freq[base + n]
            f = [field[fam, part, q, n].astype(F32) for q in range(PLANES)]
            if fam == 0:
                r = [rtab[level, q] for q in range(PLANES)]
                g = [crtab[level, q] for q in range(1, 5)]
                a0 = [f[q] * r[q] for q in range(PLANES)]
                a1 = [
                    a0[q] + g[q - 1] * (a0[q - 1] + a0[q + 1] + flat_sum(a0[q]))
                    for q in range(1, 5)
                ]
                a2 = [
                    a0[q] + g[q - 1] * (a1[q - 2] + a1[q] + flat_sum(a1[q - 1]))
                    for q in range(2, 4)
                ]
            else:
                g = [crtab[level, q] for q in range(PLANES)]
                r = [rtab[level, q] for q in range(2, 4)]
                a0 = [f[q] * g[q] for q in range(PLANES)]
                a1 = [
                    a0[q] + g[q] * (a0[q - 1] + a0[q + 1] + flat_sum(a0[q]))
                    for q in range(1, 5)
                ]
                a2 = [
                    (f[q] + (a1[q - 2] + a1[q] + flat_sum(a1[q - 1]))) * r[q - 2]
                    for q in range(2, 4)
                ]
            for k in range(2):
                turn[pl.ds(k * ROWS * PART + n, ROWS, stride=PART), :] = a2[k]
            return carry

        lax.fori_loop(0, PART, one, 0)

    def pack(c):
        for k in range(2):
            for yy in range(ROWS):
                owner = (yy % 8) // 2
                rho = k * 4 + (yy // 8) * 2 + yy % 2
                at = (k * ROWS + yy) * PART
                outbox[c, owner, rho] = turn[at : at + PART, :].astype(BF16)

    def post(c, dz, dx):
        part = c % 2
        to_x = (x + dx) % 4
        if c < 2:
            dst = dirbox.at[p, part]
            target = dev(s, ((zh + dz) % 2) * 4 + to_x)
        else:
            dst = adjbox.at[x, h, part]
            target = dev(2 * j + (h + dz) % 2, zh * 4 + to_x)
        src = outbox.at[c, to_x]
        if dz == 0 and dx == 0:
            return pltpu.make_async_copy(src, dst, post_r.at[c, 0])
        return pltpu.make_async_remote_copy(
            src_ref=src,
            dst_ref=dst,
            send_sem=post_s.at[c, dz * 4 + dx],
            recv_sem=post_r.at[c, dz * 4 + dx],
            device_id=target,
            device_id_type=MESH,
        )

    def post_arrival(c, dz, dx):
        part = c % 2
        from_x = (x + 4 - dx) % 4
        if c < 2:
            dst = dirbox.at[((zh + dz) % 2) * 4 + from_x, part]
        else:
            dst = adjbox.at[from_x, (h + dz) % 2, part]
        pltpu.make_async_remote_copy(
            src_ref=outbox.at[c, 0],
            dst_ref=dst,
            send_sem=post_s.at[c, 0],
            recv_sem=post_r.at[c, dz * 4 + dx],
            device_id=dev(s, p),
            device_id_type=MESH,
        ).wait_recv()

    far_first = [(dz, dx) for dz in (1, 0) for dx in (2, 1, 3, 0)]
    for c in range(4):
        halo_own(c).wait()
        from_neighbours(halo_arrival(c))
        smooth(c // 2, c % 2)
        pack(c)
        for dz, dx in far_first:
            post(c, dz, dx).start()

    lcopy.wait()
    rcopy.wait()
    inv_root = 1.0 / jnp.sqrt(sing[...])
    left_s = (lbuf[...].reshape(512, 64) * inv_root).astype(BF16)
    right_s = (rbuf[...].reshape(512, 64) * inv_root).astype(BF16)

    def arrived(c):
        for dz, dx in far_first:
            if dz == 0 and dx == 0:
                post(c, 0, 0).wait()
            else:
                post_arrival(c, dz, dx)

    for c in range(4):
        arrived(c)

    def adj_rows(xx):
        pieces = [
            jnp.concatenate([adjbox[xx, hh, part, rho] for rho in range(8)], axis=1)
            for hh in range(2)
            for part in range(2)
        ]
        return jnp.concatenate(pieces, axis=0)

    adj_all = [adj_rows((x + dx) % 4) for dx in range(4)]

    def sa_copy(dy, dx):
        return pltpu.make_async_remote_copy(
            src_ref=psend.at[dy * 4 + dx],
            dst_ref=precv.at[dy * 4 + dx],
            send_sem=sa_s.at[dy * 4 + dx],
            recv_sem=sa_r.at[dy * 4 + dx],
            device_id=dev(2 * (zl * 4 + (y + dy) % 4) + h, zh * 4 + (x + dx) % 4),
            device_id_type=MESH,
        )

    for dy in (2, 1, 3, 0):
        yy = (y + dy) % 4
        pieces = [
            jnp.concatenate([dirbox[2 * zz + yy // 2, yy % 2, rho] for rho in range(8)], axis=1)
            for zz in range(4)
        ]
        dir_y = jnp.concatenate(pieces, axis=0)
        for dx in (2, 1, 3, 0):
            block = contract_last(dir_y, adj_all[dx])
            if dy == 0 and dx == 0:
                gsum[...] = block
            else:
                psend[dy * 4 + dx] = block.astype(BF16)
                sa_copy(dy, dx).start()

    def dir_cells(k, t):
        rho = k * 4 + 2 * zh + t
        return jnp.concatenate(
            [dirbox[pp, part, rho] for pp in range(8) for part in range(2)], axis=0
        )

    def adj_cells(zz, t):
        rho = h * 4 + 2 * zz + t
        return jnp.concatenate(
            [adjbox[xx, hh, part, rho] for xx in range(4) for hh in range(2) for part in range(2)],
            axis=0,
        )

    for t in range(2):
        mpart[0, t] = contract_first(right_s, dir_cells(1 - h, t))
        mpart[1, t] = contract_first(left_s, adj_cells(1 - zh, t))

    def md_copy(fam):
        target = dev(2 * j + 1 - h, p) if fam == 0 else dev(s, (1 - zh) * 4 + x)
        return pltpu.make_async_remote_copy(
            src_ref=mpart.at[fam],
            dst_ref=mrecv.at[fam],
            send_sem=md_s.at[fam],
            recv_sem=md_r.at[fam],
            device_id=target,
            device_id_type=MESH,
        )

    for fam in range(2):
        md_copy(fam).start()
    own_d = [contract_first(right_s, dir_cells(h, t)) for t in range(2)]
    own_a = [contract_first(left_s, adj_cells(zh, t)) for t in range(2)]

    for dy in (1, 3, 2, 0):
        for dx in (1, 3, 2, 0):
            if dy or dx:
                sa_copy(dy, dx).wait_recv()
    total = gsum[...]
    for i in range(1, 16):
        total = total + precv[i].astype(F32)
    for zz in range(4):
        bsend[zz] = total[zz * 32 : zz * 32 + 32]

    def sb_copy(dz):
        return pltpu.make_async_remote_copy(
            src_ref=bsend.at[(zl + dz) % 4],
            dst_ref=brecv.at[dz],
            send_sem=sb_s.at[dz],
            recv_sem=sb_r.at[dz],
            device_id=dev(2 * (((zl + dz) % 4) * 4 + y) + h, p),
            device_id_type=MESH,
        )

    for dz in (2, 1, 3):
        sb_copy(dz).start()

    for fam in range(2):
        md_copy(fam).wait_recv()
    for t in range(2):
        dm_o[:, t, :] = own_d[t] + mrecv[0, t]
        am_o[:, t, :] = own_a[t] + mrecv[1, t]

    for dz in (1, 3, 2):
        sb_copy(dz).wait_recv()
    mine = bsend[zl] + brecv[1] + brecv[2] + brecv[3]
    gram_o[...] = (mine * weight).T

    to_neighbours(lambda dj, half: cond_copy(dj, half).wait_send())
    for c in range(4):
        to_neighbours(lambda dj, half: halo_copy(c, dj, half).wait_send())
        for dz, dx in far_first:
            if dz or dx:
                post(c, dz, dx).wait_send()
    for dy in range(4):
        for dx in range(4):
            if dy or dx:
                sa_copy(dy, dx).wait_send()
    for dz in range(1, 4):
        sb_copy(dz).wait_send()
    for fam in range(2):
        md_copy(fam).wait_send()


def per_device(
    forcing_direct,
    forcing_adjoint,
    conductance,
    shift_table,
    freq_direct,
    freq_adjoint,
    left_factors,
    right_factors,
    singular_values,
):
    weight = 1.0 / math.sqrt(32 * ROWS * LANES)
    any_ = pl.BlockSpec(memory_space=pl.ANY)
    vmem = pl.BlockSpec(memory_space=pltpu.VMEM)
    smem = pl.BlockSpec(memory_space=pltpu.SMEM)
    dma = pltpu.SemaphoreType.DMA
    gram, direct_modes, adjoint_modes = pl.pallas_call(
        functools.partial(kernel, weight),
        out_shape=(
            jax.ShapeDtypeStruct((128, 32), F32),
            jax.ShapeDtypeStruct((64, 2, LANES), F32),
            jax.ShapeDtypeStruct((64, 2, LANES), F32),
        ),
        in_specs=[any_, any_, any_, smem, smem, smem, any_, any_, vmem],
        out_specs=(vmem, vmem, vmem),
        scratch_shapes=[
            pltpu.VMEM((2, 2, PLANES, PART, ROWS, LANES), BF16),
            pltpu.VMEM((PLANES, ROWS, LANES), F32),
            pltpu.VMEM((LEVELS, PLANES, ROWS, LANES), F32),
            pltpu.VMEM((LEVELS, PLANES, ROWS, LANES), F32),
            pltpu.VMEM((2 * ROWS * PART, LANES), F32),
            pltpu.VMEM((4, 4, 8, PART, LANES), BF16),
            pltpu.VMEM((8, 2, 8, PART, LANES), BF16),
            pltpu.VMEM((4, 2, 2, 8, PART, LANES), BF16),
            pltpu.VMEM((16, 128, 128), BF16),
            pltpu.VMEM((16, 128, 128), BF16),
            pltpu.VMEM((128, 128), F32),
            pltpu.VMEM((4, 32, 128), F32),
            pltpu.VMEM((4, 32, 128), F32),
            pltpu.VMEM((2, 2, 64, LANES), F32),
            pltpu.VMEM((2, 2, 64, LANES), F32),
            pltpu.VMEM((4, 128, 64), F32),
            pltpu.VMEM((8, 2, PART, 64), F32),
            dma((4, 6)), dma((4, 6)),
            dma((6,)), dma((6,)),
            dma((7,)),
            dma((4, 8)), dma((4, 8)),
            dma((16,)), dma((16,)),
            dma((4,)), dma((4,)),
            dma((2,)), dma((2,)),
        ],
        compiler_params=pltpu.CompilerParams(
            collective_id=0, has_side_effects=True, vmem_limit_bytes=48 * 1024 * 1024
        ),
        name="window",
    )(
        forcing_direct.reshape(128, ROWS, LANES),
        forcing_adjoint.reshape(128, ROWS, LANES),
        conductance.reshape(ROWS, LANES),
        shift_table,
        freq_direct,
        freq_adjoint,
        left_factors.reshape(8, 128, 64),
        right_factors.reshape(8, 2, 2, PART, 64),
        singular_values.reshape(1, 64),
    )
    return (
        gram,
        direct_modes.reshape(64, 1, 2, LANES),
        adjoint_modes.reshape(64, 1, 2, LANES),
    )


def solution(mesh):
    placed = (
        P("snap", "space", None, None),
        P("snap", "space", None, None),
        P("space", None, None),
        P(),
        P("snap"),
        P("snap"),
        P(),
        P(),
        P(),
    )
    return jax.shard_map(
        per_device,
        mesh=mesh,
        in_specs=placed,
        out_specs=(
            P("snap", "space"),
            P(None, "space", "snap", None),
            P(None, "space", "snap", None),
        ),
        check_vma=False,
    )
```

```python
import functools
import math

import jax
import jax.numpy as jnp
from jax import lax
from jax.experimental import pallas as pl
from jax.experimental.pallas import tpu as pltpu
from jax.sharding import PartitionSpec as P

MESH = pl.DeviceIdType.MESH
F32 = jnp.float32
BF16 = jnp.bfloat16

ROWS = 16
LANES = 128
PLANES = 6
PART = 32
LEVELS = 16
UNROLL = 4


def contract_last(a, b):
    return lax.dot_general(a, b, (((1,), (1,)), ((), ())), preferred_element_type=F32)


def product(a, b):
    return lax.dot_general(a, b, (((1,), (0,)), ((), ())), preferred_element_type=F32)


def kernel(
    weight,
    fd, fa, cond, table, freq_d, freq_a, left, right, sing,
    gram_o, dm_o, am_o,
    field, chalo, rtab, crtab, turn, outbox, dirbox, adjbox,
    psend, precv, gsum, bsend, brecv, mpart, mrecv, lbuf, rbuf, rscaled,
    halo_s, halo_r, cond_s, cond_r, load_s, post_s, post_r, sa_s, sa_r, sb_s, sb_r, md_s, md_r,
):
    s = lax.axis_index("space")
    p = lax.axis_index("snap")
    j, h = s // 2, s % 2
    zl, y = j // 4, j % 4
    zh, x = p // 4, p % 4
    forcing = (fd, fa)

    def dev(ss, pp):
        return (ss, pp)

    barrier = pltpu.get_barrier_semaphore()
    greet = [dev(2 * j + 1 - h, p)]
    for dj in (-1, 1):
        for dh in (0, 1):
            greet.append(dev(2 * ((j + dj + 16) % 16) + dh, p))
    for dz in range(2):
        for dx in range(4):
            if dz or dx:
                greet.append(dev(s, ((zh + dz) % 2) * 4 + (x + dx) % 4))
    for dx in range(1, 4):
        greet.append(dev(2 * j + 1 - h, zh * 4 + (x + dx) % 4))
    for dy in range(1, 4):
        for dx in range(4):
            greet.append(dev(2 * (zl * 4 + (y + dy) % 4) + h, zh * 4 + (x + dx) % 4))
    for dz in range(1, 4):
        greet.append(dev(2 * (((zl + dz) % 4) * 4 + y) + h, p))
    for target in greet:
        pl.semaphore_signal(barrier, inc=1, device_id=target, device_id_type=MESH)
    pl.semaphore_wait(barrier, len(greet))

    def start_row(fam, part, half):
        return part * 64 + half * 32 if fam == 0 else half * 64 + part * 32

    def halo_copy(c, dj, half):
        fam, part = c // 2, c % 2
        slot = 2 * (dj + 1)
        return pltpu.make_async_remote_copy(
            src_ref=forcing[fam].at[pl.ds(start_row(fam, part, half), PART)],
            dst_ref=field.at[fam, part, 2 * (1 - dj) + h],
            send_sem=halo_s.at[c, slot + half],
            recv_sem=halo_r.at[c, 2 * (1 - dj) + h],
            device_id=dev(2 * (j + dj) + half, p),
            device_id_type=MESH,
        )

    def halo_own(c):
        fam, part = c // 2, c % 2
        return pltpu.make_async_copy(
            forcing[fam].at[pl.ds(start_row(fam, part, h), PART)],
            field.at[fam, part, 2 + h],
            load_s.at[c],
        )

    def cond_copy(dj, half):
        return pltpu.make_async_remote_copy(
            src_ref=cond,
            dst_ref=chalo.at[2 * (1 - dj) + h],
            send_sem=cond_s.at[2 * (dj + 1) + half],
            recv_sem=cond_r.at[2 * (1 - dj) + h],
            device_id=dev(2 * (j + dj) + half, p),
            device_id_type=MESH,
        )

    def to_neighbours(act):
        for dj, inside in ((1, j < 15), (-1, j > 0)):
            @pl.when(inside)
            def _():
                for half in range(2):
                    act(dj, half)
        act(0, 1 - h)

    def from_neighbours(act):
        for dj, inside in ((-1, j > 0), (1, j < 15)):
            @pl.when(inside)
            def _():
                for half in range(2):
                    act(dj, half)
        act(0, 1 - h)

    to_neighbours(lambda dj, half: cond_copy(dj, half).start())
    for c in range(4):
        to_neighbours(lambda dj, half: halo_copy(c, dj, half).start())
        halo_own(c).start()
    lcopy = pltpu.make_async_copy(left.at[:, pl.ds(pl.multiple_of(zh * 512, 512), 512)], lbuf, load_s.at[4])
    rcopy = pltpu.make_async_copy(right, rbuf, load_s.at[5])
    ccopy = pltpu.make_async_copy(cond, chalo.at[2 + h], load_s.at[6])
    lcopy.start()
    rcopy.start()
    ccopy.start()

    for first, edge in ((0, j == 0), (4, j == 15)):
        @pl.when(edge)
        def _():
            for k in range(2):
                chalo[first + k] = jnp.ones((ROWS, LANES), F32)
                for fam in range(2):
                    for part in range(2):
                        field[fam, part, first + k] = jnp.zeros((PART, ROWS, LANES), BF16)

    def cond_arrival(dj, half):
        pltpu.make_async_remote_copy(
            src_ref=cond,
            dst_ref=chalo.at[2 * (1 + dj) + half],
            send_sem=cond_s.at[0],
            recv_sem=cond_r.at[2 * (1 + dj) + half],
            device_id=dev(s, p),
            device_id_type=MESH,
        ).wait_recv()

    def halo_arrival(c):
        fam, part = c // 2, c % 2

        def act(dj, half):
            pltpu.make_async_remote_copy(
                src_ref=forcing[fam].at[pl.ds(0, PART)],
                dst_ref=field.at[fam, part, 2 * (1 + dj) + half],
                send_sem=halo_s.at[c, 0],
                recv_sem=halo_r.at[c, 2 * (1 + dj) + half],
                device_id=dev(s, p),
                device_id_type=MESH,
            ).wait_recv()

        return act

    ccopy.wait()
    from_neighbours(cond_arrival)

    def fill(level, carry):
        shift = table[level]
        for q in range(PLANES):
            there = j + (q // 2 - 1)
            mask = jnp.where((there >= 0) & (there < 16), F32(1.0), F32(0.0))
            coeff = chalo[q]
            inverse = mask / (shift + 6.0 * coeff)
            rtab[level, q] = inverse
            crtab[level, q] = coeff * inverse
        return carry

    lax.fori_loop(0, LEVELS, fill, 0)

    row = lax.broadcasted_iota(jnp.int32, (ROWS, LANES), 0)
    lane = lax.broadcasted_iota(jnp.int32, (ROWS, LANES), 1)

    def flat_sum(v):
        up = jnp.where(row == 0, 0.0, pltpu.roll(v, 1, 0))
        down = jnp.where(row == ROWS - 1, 0.0, pltpu.roll(v, ROWS - 1, 0))
        fore = jnp.where(lane == 0, 0.0, pltpu.roll(v, 1, 1))
        aft = jnp.where(lane == LANES - 1, 0.0, pltpu.roll(v, LANES - 1, 1))
        return (up + down) + (fore + aft)

    def smooth(fam, part):
        freq = freq_d if fam == 0 else freq_a
        base = start_row(fam, part, h)

        def one(n, carry):
            level = freq[base + n]
            f = [field[fam, part, q, n].astype(F32) for q in range(PLANES)]
            if fam == 0:
                r = [rtab[level, q] for q in range(PLANES)]
                g = [crtab[level, q] for q in range(1, 5)]
                a0 = [f[q] * r[q] for q in range(PLANES)]
                a1 = [
                    a0[q] + g[q - 1] * (a0[q - 1] + a0[q + 1] + flat_sum(a0[q]))
                    for q in range(1, 5)
                ]
                a2 = [
                    a0[q] + g[q - 1] * (a1[q - 2] + a1[q] + flat_sum(a1[q - 1]))
                    for q in range(2, 4)
                ]
            else:
                g = [crtab[level, q] for q in range(PLANES)]
                r = [rtab[level, q] for q in range(2, 4)]
                a0 = [f[q] * g[q] for q in range(PLANES)]
                a1 = [
                    a0[q] + g[q] * (a0[q - 1] + a0[q + 1] + flat_sum(a0[q]))
                    for q in range(1, 5)
                ]
                a2 = [
                    (f[q] + (a1[q - 2] + a1[q] + flat_sum(a1[q - 1]))) * r[q - 2]
                    for q in range(2, 4)
                ]
            for k in range(2):
                turn[pl.ds(k * ROWS * PART + n, ROWS, stride=PART), :] = a2[k]
            return carry

        lax.fori_loop(0, PART, one, 0, unroll=UNROLL)

    def pack(c):
        for k in range(2):
            for yy in range(ROWS):
                owner = (yy % 8) // 2
                rho = k * 4 + (yy // 8) * 2 + yy % 2
                at = (k * ROWS + yy) * PART
                outbox[c, owner, rho] = turn[at : at + PART, :].astype(BF16)

    def post(c, dz, dx):
        part = c % 2
        to_x = (x + dx) % 4
        if c < 2:
            dst = dirbox.at[p, part]
            target = dev(s, ((zh + dz) % 2) * 4 + to_x)
        else:
            dst = adjbox.at[x, h, part]
            target = dev(2 * j + (h + dz) % 2, zh * 4 + to_x)
        src = outbox.at[c, to_x]
        if dz == 0 and dx == 0:
            return pltpu.make_async_copy(src, dst, post_r.at[c, 0])
        return pltpu.make_async_remote_copy(
            src_ref=src,
            dst_ref=dst,
            send_sem=post_s.at[c, dz * 4 + dx],
            recv_sem=post_r.at[c, dz * 4 + dx],
            device_id=target,
            device_id_type=MESH,
        )

    def post_arrival(c, dz, dx):
        part = c % 2
        from_x = (x + 4 - dx) % 4
        if c < 2:
            dst = dirbox.at[((zh + dz) % 2) * 4 + from_x, part]
        else:
            dst = adjbox.at[from_x, (h + dz) % 2, part]
        pltpu.make_async_remote_copy(
            src_ref=outbox.at[c, 0],
            dst_ref=dst,
            send_sem=post_s.at[c, 0],
            recv_sem=post_r.at[c, dz * 4 + dx],
            device_id=dev(s, p),
            device_id_type=MESH,
        ).wait_recv()

    far_first = [(dz, dx) for dz in (1, 0) for dx in (2, 1, 3, 0)]
    for c in range(4):
        halo_own(c).wait()
        from_neighbours(halo_arrival(c))
        smooth(c // 2, c % 2)
        pack(c)
        for dz, dx in far_first:
            post(c, dz, dx).start()

    lcopy.wait()
    rcopy.wait()
    inv_root = jnp.broadcast_to(1.0 / jnp.sqrt(sing[...]), (64, 64))
    across = lax.broadcasted_iota(jnp.int32, (64, 64), 1)
    along = lax.broadcasted_iota(jnp.int32, (64, 64), 0)
    inv_root = jnp.sum(jnp.where(across == along, inv_root, 0.0), axis=1, keepdims=True)
    left_s = (lbuf[...] * inv_root).astype(BF16)
    scaled = rbuf[...] * inv_root
    scaled = jnp.where(h == 1, pltpu.roll(scaled, 1024 - PART, 1), scaled)
    for zz in range(2):
        rscaled[zz] = jnp.concatenate(
            [scaled[:, q * 64 : q * 64 + PART] for q in range(zz * 8, zz * 8 + 8)], axis=1
        ).astype(BF16)

    def arrived(c, dz):
        for dx in (2, 1, 3, 0):
            if dz == 0 and dx == 0:
                post(c, 0, 0).wait()
            else:
                post_arrival(c, dz, dx)

    def adj_rows(dx):
        xx = (x + dx) % 4
        pieces = [
            jnp.concatenate([adjbox[xx, hh, part, rho] for rho in range(8)], axis=1)
            for hh in range(2)
            for part in range(2)
        ]
        return jnp.concatenate(pieces, axis=0)

    def dir_rows(zz, yy, part):
        pieces = [
            jnp.concatenate(
                [dirbox[4 * zz + 2 * t + yy // 2, part, rho] for rho in range(8)], axis=1
            )
            for t in range(2)
        ]
        return jnp.concatenate(pieces, axis=0)

    def sa_copy(half, dy, dx):
        return pltpu.make_async_remote_copy(
            src_ref=psend.at[half, dy * 4 + dx],
            dst_ref=precv.at[half, dy * 4 + dx],
            send_sem=sa_s.at[half, dy * 4 + dx],
            recv_sem=sa_r.at[half, dy * 4 + dx],
            device_id=dev(2 * (zl * 4 + (y + dy) % 4) + h, zh * 4 + (x + dx) % 4),
            device_id_type=MESH,
        )

    def ship(half, dy, dx, block):
        psend[half, dy * 4 + dx] = block.astype(BF16)
        sa_copy(half, dy, dx).start()

    arrived(0, 0)
    arrived(1, 0)
    arrived(2, 1)
    arrived(2, 0)
    arrived(3, 1)
    arrived(3, 0)
    turns = (2, 1, 3, 0)
    dir_own = jnp.concatenate(
        [dir_rows(zh, (y + dy) % 4, (y + dy) % 2) for dy in turns], axis=0
    )
    for dx in turns:
        block = contract_last(dir_own, adj_rows(dx))
        for i, dy in enumerate(turns):
            if dx == 0 and dy == 0:
                gsum[0] = block[64 * i : 64 * i + 64]
            else:
                ship(0, dy, dx, block[64 * i : 64 * i + 64])

    def dir_cells(zz, k, t):
        rho = k * 4 + 2 * zh + t
        return jnp.concatenate(
            [dirbox[4 * zz + i, part, rho] for i in range(4) for part in range(2)], axis=0
        )

    def adj_cells(zz, t):
        rho = h * 4 + 2 * zz + t
        return jnp.concatenate(
            [adjbox[xx, hh, part, rho] for xx in range(4) for hh in range(2) for part in range(2)],
            axis=0,
        )

    def md_copy(fam):
        target = dev(2 * j + 1 - h, p) if fam == 0 else dev(s, (1 - zh) * 4 + x)
        return pltpu.make_async_remote_copy(
            src_ref=mpart.at[fam],
            dst_ref=mrecv.at[fam],
            send_sem=md_s.at[fam],
            recv_sem=md_r.at[fam],
            device_id=target,
            device_id_type=MESH,
        )

    for t in range(2):
        mpart[1, t] = product(left_s, adj_cells(1 - zh, t))
    md_copy(1).start()
    for t in range(2):
        mpart[0, t] = product(rscaled[zh], dir_cells(zh, 1 - h, t))
        dm_o[:, t, :] = product(rscaled[zh], dir_cells(zh, h, t))
        am_o[:, t, :] = product(left_s, adj_cells(zh, t))

    def other_half(part):
        first = dir_rows(1 - zh, part, part)
        second = dir_rows(1 - zh, 2 + part, part)
        rows = jnp.concatenate([first, second], axis=0)
        for dx in turns:
            block = contract_last(rows, adj_rows(dx))
            for i in range(2):
                piece = block[64 * i : 64 * i + 64]
                dy = (2 * i + part - y + 4) % 4
                if dx:
                    ship(1, dy, dx, piece)
                else:
                    @pl.when(dy == 0)
                    def _():
                        gsum[1] = piece

                    @pl.when(dy != 0)
                    def _():
                        ship(1, dy, dx, piece)

    def sb_copy(dz):
        return pltpu.make_async_remote_copy(
            src_ref=bsend.at[(zl + dz) % 4],
            dst_ref=brecv.at[dz],
            send_sem=sb_s.at[dz],
            recv_sem=sb_r.at[dz],
            device_id=dev(2 * (((zl + dz) % 4) * 4 + y) + h, p),
            device_id_type=MESH,
        )

    def add_up(half):
        for dy in (1, 3, 2, 0):
            for dx in (1, 3, 2, 0):
                if dy or dx:
                    sa_copy(half, dy, dx).wait_recv()
        total = gsum[half]
        for i in range(1, 16):
            total = total + precv[half, i].astype(F32)
        zz = zh if half == 0 else 1 - zh
        for t in range(2):
            bsend[2 * zz + t] = total[t * 32 : t * 32 + 32]
        for dz in (2, 1, 3):
            @pl.when(((zl + dz) % 4) // 2 == zz)
            def _():
                sb_copy(dz).start()

    arrived(0, 1)
    other_half(0)
    add_up(0)
    arrived(1, 1)
    other_half(1)
    for t in range(2):
        mpart[0, t] = mpart[0, t] + product(rscaled[1 - zh], dir_cells(1 - zh, 1 - h, t))
    md_copy(0).start()
    for t in range(2):
        dm_o[:, t, :] = dm_o[:, t, :] + product(rscaled[1 - zh], dir_cells(1 - zh, h, t))
    md_copy(1).wait_recv()
    for t in range(2):
        am_o[:, t, :] = am_o[:, t, :] + mrecv[1, t]
    add_up(1)
    md_copy(0).wait_recv()
    for t in range(2):
        dm_o[:, t, :] = dm_o[:, t, :] + mrecv[0, t]
    for dz in (1, 3, 2):
        sb_copy(dz).wait_recv()
    gram_o[...] = (bsend[zl] + brecv[1] + brecv[2] + brecv[3]) * weight

    to_neighbours(lambda dj, half: cond_copy(dj, half).wait_send())
    for c in range(4):
        to_neighbours(lambda dj, half: halo_copy(c, dj, half).wait_send())
        for dz, dx in far_first:
            if dz or dx:
                post(c, dz, dx).wait_send()
    for dy in range(4):
        for dx in range(4):
            if dy or dx:
                sa_copy(0, dy, dx).wait_send()
                sa_copy(1, dy, dx).wait_send()
    for dz in range(1, 4):
        sb_copy(dz).wait_send()
    for fam in range(2):
        md_copy(fam).wait_send()


def per_device(
    forcing_direct,
    forcing_adjoint,
    conductance,
    shift_table,
    freq_direct,
    freq_adjoint,
    left_factors,
    right_factors,
    singular_values,
):
    weight = 1.0 / math.sqrt(32 * ROWS * LANES)
    any_ = pl.BlockSpec(memory_space=pltpu.HBM)
    vmem = pl.BlockSpec(memory_space=pltpu.VMEM)
    smem = pl.BlockSpec(memory_space=pltpu.SMEM)
    dma = pltpu.SemaphoreType.DMA
    gram, direct_modes, adjoint_modes = pl.pallas_call(
        functools.partial(kernel, weight),
        out_shape=(
            jax.ShapeDtypeStruct((32, 128), F32),
            jax.ShapeDtypeStruct((64, 2, LANES), F32),
            jax.ShapeDtypeStruct((64, 2, LANES), F32),
        ),
        in_specs=[any_, any_, any_, smem, smem, smem, any_, any_, vmem],
        out_specs=(vmem, vmem, vmem),
        scratch_shapes=[
            pltpu.VMEM((2, 2, PLANES, PART, ROWS, LANES), BF16),
            pltpu.VMEM((PLANES, ROWS, LANES), F32),
            pltpu.VMEM((LEVELS, PLANES, ROWS, LANES), F32),
            pltpu.VMEM((LEVELS, PLANES, ROWS, LANES), F32),
            pltpu.VMEM((2 * ROWS * PART, LANES), F32),
            pltpu.VMEM((4, 4, 8, PART, LANES), BF16),
            pltpu.VMEM((8, 2, 8, PART, LANES), BF16),
            pltpu.VMEM((4, 2, 2, 8, PART, LANES), BF16),
            pltpu.VMEM((2, 16, 64, 128), BF16),
            pltpu.VMEM((2, 16, 64, 128), BF16),
            pltpu.VMEM((2, 64, 128), F32),
            pltpu.VMEM((4, 32, 128), F32),
            pltpu.VMEM((4, 32, 128), F32),
            pltpu.VMEM((2, 2, 64, LANES), F32),
            pltpu.VMEM((2, 2, 64, LANES), F32),
            pltpu.VMEM((64, 512), F32),
            pltpu.VMEM((64, 1024), F32),
            pltpu.VMEM((2, 64, 256), BF16),
            dma((4, 6)), dma((4, 6)),
            dma((6,)), dma((6,)),
            dma((7,)),
            dma((4, 8)), dma((4, 8)),
            dma((2, 16)), dma((2, 16)),
            dma((4,)), dma((4,)),
            dma((2,)), dma((2,)),
        ],
        compiler_params=pltpu.CompilerParams(
            collective_id=0, has_side_effects=True, vmem_limit_bytes=63 * 1024 * 1024
        ),
        name="window",
    )(
        forcing_direct.reshape(128, ROWS, LANES),
        forcing_adjoint.reshape(128, ROWS, LANES),
        conductance.reshape(ROWS, LANES),
        shift_table,
        freq_direct,
        freq_adjoint,
        left_factors.T,
        right_factors.T,
        singular_values.reshape(1, 64),
    )
    return (
        gram.T,
        direct_modes.reshape(64, 1, 2, LANES),
        adjoint_modes.reshape(64, 1, 2, LANES),
    )


def solution(mesh):
    placed = (
        P("snap", "space", None, None),
        P("snap", "space", None, None),
        P("space", None, None),
        P(),
        P("snap"),
        P("snap"),
        P(),
        P(),
        P(),
    )
    return jax.shard_map(
        per_device,
        mesh=mesh,
        in_specs=placed,
        out_specs=(
            P("snap", "space"),
            P(None, "space", "snap", None),
            P(None, "space", "snap", None),
        ),
        check_vma=False,
    )
```

```python
import functools
import math

import jax
import jax.numpy as jnp
from jax import lax
from jax.experimental import pallas as pl
from jax.experimental.pallas import tpu as pltpu
from jax.sharding import PartitionSpec as P

MESH = pl.DeviceIdType.MESH
F32 = jnp.float32
BF16 = jnp.bfloat16

ROWS = 16
LANES = 128
PLANES = 6
PART = 32
LEVELS = 16
UNROLL = 4


def contract_last(a, b):
    return lax.dot_general(a, b, (((1,), (1,)), ((), ())), preferred_element_type=F32)


def product(a, b):
    return lax.dot_general(a, b, (((1,), (0,)), ((), ())), preferred_element_type=F32)


def kernel(
    weight,
    fd, fa, cond, table, freq_d, freq_a, left, right, sing,
    gram_o, dm_o, am_o,
    field, chalo, rtab, crtab, turn, outbox, dirbox, adjbox,
    psend, precv, gsum, bsend, brecv, mpart, mrecv, lbuf, rbuf, rscaled,
    halo_s, halo_r, cond_s, cond_r, load_s, post_s, post_r, sa_s, sa_r, sb_s, sb_r, md_s, md_r,
):
    s = lax.axis_index("space")
    p = lax.axis_index("snap")
    j, h = s // 2, s % 2
    zl, y = j // 4, j % 4
    zh, x = p // 4, p % 4
    forcing = (fd, fa)

    def dev(ss, pp):
        return (ss, pp)

    barrier = pltpu.get_barrier_semaphore()
    greet = [dev(2 * j + 1 - h, p)]
    for dj in (-1, 1):
        for dh in (0, 1):
            greet.append(dev(2 * ((j + dj + 16) % 16) + dh, p))
    for dz in range(2):
        for dx in range(4):
            if dz or dx:
                greet.append(dev(s, ((zh + dz) % 2) * 4 + (x + dx) % 4))
    for dx in range(1, 4):
        greet.append(dev(2 * j + 1 - h, zh * 4 + (x + dx) % 4))
    for dy in range(1, 4):
        for dx in range(4):
            greet.append(dev(2 * (zl * 4 + (y + dy) % 4) + h, zh * 4 + (x + dx) % 4))
    for dz in range(1, 4):
        greet.append(dev(2 * (((zl + dz) % 4) * 4 + y) + h, p))
    for target in greet:
        pl.semaphore_signal(barrier, inc=1, device_id=target, device_id_type=MESH)
    pl.semaphore_wait(barrier, len(greet))

    def start_row(fam, part, half):
        return part * 64 + half * 32 if fam == 0 else half * 64 + part * 32

    def halo_copy(c, dj, half):
        fam, part = c // 2, c % 2
        slot = 2 * (dj + 1)
        return pltpu.make_async_remote_copy(
            src_ref=forcing[fam].at[pl.ds(start_row(fam, part, half), PART)],
            dst_ref=field.at[fam, part, 2 * (1 - dj) + h],
            send_sem=halo_s.at[c, slot + half],
            recv_sem=halo_r.at[c, 2 * (1 - dj) + h],
            device_id=dev(2 * (j + dj) + half, p),
            device_id_type=MESH,
        )

    def halo_own(c):
        fam, part = c // 2, c % 2
        return pltpu.make_async_copy(
            forcing[fam].at[pl.ds(start_row(fam, part, h), PART)],
            field.at[fam, part, 2 + h],
            load_s.at[c],
        )

    def cond_copy(dj, half):
        return pltpu.make_async_remote_copy(
            src_ref=cond,
            dst_ref=chalo.at[2 * (1 - dj) + h],
            send_sem=cond_s.at[2 * (dj + 1) + half],
            recv_sem=cond_r.at[2 * (1 - dj) + h],
            device_id=dev(2 * (j + dj) + half, p),
            device_id_type=MESH,
        )

    def to_neighbours(act):
        for dj, inside in ((1, j < 15), (-1, j > 0)):
            @pl.when(inside)
            def _():
                for half in range(2):
                    act(dj, half)
        act(0, 1 - h)

    def from_neighbours(act):
        for dj, inside in ((-1, j > 0), (1, j < 15)):
            @pl.when(inside)
            def _():
                for half in range(2):
                    act(dj, half)
        act(0, 1 - h)

    to_neighbours(lambda dj, half: cond_copy(dj, half).start())
    for c in range(4):
        to_neighbours(lambda dj, half: halo_copy(c, dj, half).start())
        halo_own(c).start()
    lcopy = pltpu.make_async_copy(left.at[:, pl.ds(pl.multiple_of(zh * 512, 512), 512)], lbuf, load_s.at[4])
    rcopy = pltpu.make_async_copy(right, rbuf, load_s.at[5])
    ccopy = pltpu.make_async_copy(cond, chalo.at[2 + h], load_s.at[6])
    lcopy.start()
    rcopy.start()
    ccopy.start()

    for first, edge in ((0, j == 0), (4, j == 15)):
        @pl.when(edge)
        def _():
            for k in range(2):
                chalo[first + k] = jnp.ones((ROWS, LANES), F32)
                for fam in range(2):
                    for part in range(2):
                        field[fam, part, first + k] = jnp.zeros((PART, ROWS, LANES), BF16)

    def cond_arrival(dj, half):
        pltpu.make_async_remote_copy(
            src_ref=cond,
            dst_ref=chalo.at[2 * (1 + dj) + half],
            send_sem=cond_s.at[0],
            recv_sem=cond_r.at[2 * (1 + dj) + half],
            device_id=dev(s, p),
            device_id_type=MESH,
        ).wait_recv()

    def halo_arrival(c):
        fam, part = c // 2, c % 2

        def act(dj, half):
            pltpu.make_async_remote_copy(
                src_ref=forcing[fam].at[pl.ds(0, PART)],
                dst_ref=field.at[fam, part, 2 * (1 + dj) + half],
                send_sem=halo_s.at[c, 0],
                recv_sem=halo_r.at[c, 2 * (1 + dj) + half],
                device_id=dev(s, p),
                device_id_type=MESH,
            ).wait_recv()

        return act

    ccopy.wait()
    from_neighbours(cond_arrival)

    def fill(level, carry):
        shift = table[level]
        for q in range(PLANES):
            there = j + (q // 2 - 1)
            mask = jnp.where((there >= 0) & (there < 16), F32(1.0), F32(0.0))
            coeff = chalo[q]
            inverse = mask / (shift + 6.0 * coeff)
            rtab[level, q] = inverse
            crtab[level, q] = coeff * inverse
        return carry

    lax.fori_loop(0, LEVELS, fill, 0)

    row = lax.broadcasted_iota(jnp.int32, (ROWS, LANES), 0)
    lane = lax.broadcasted_iota(jnp.int32, (ROWS, LANES), 1)

    def flat_sum(v):
        up = jnp.where(row == 0, 0.0, pltpu.roll(v, 1, 0))
        down = jnp.where(row == ROWS - 1, 0.0, pltpu.roll(v, ROWS - 1, 0))
        fore = jnp.where(lane == 0, 0.0, pltpu.roll(v, 1, 1))
        aft = jnp.where(lane == LANES - 1, 0.0, pltpu.roll(v, LANES - 1, 1))
        return (up + down) + (fore + aft)

    def smooth(fam, part):
        freq = freq_d if fam == 0 else freq_a
        base = start_row(fam, part, h)

        def one(n, carry):
            level = freq[base + n]
            f = [field[fam, part, q, n].astype(F32) for q in range(PLANES)]
            if fam == 0:
                r = [rtab[level, q] for q in range(PLANES)]
                g = [crtab[level, q] for q in range(1, 5)]
                a0 = [f[q] * r[q] for q in range(PLANES)]
                a1 = [
                    a0[q] + g[q - 1] * (a0[q - 1] + a0[q + 1] + flat_sum(a0[q]))
                    for q in range(1, 5)
                ]
                a2 = [
                    a0[q] + g[q - 1] * (a1[q - 2] + a1[q] + flat_sum(a1[q - 1]))
                    for q in range(2, 4)
                ]
            else:
                g = [crtab[level, q] for q in range(PLANES)]
                r = [rtab[level, q] for q in range(2, 4)]
                a0 = [f[q] * g[q] for q in range(PLANES)]
                a1 = [
                    a0[q] + g[q] * (a0[q - 1] + a0[q + 1] + flat_sum(a0[q]))
                    for q in range(1, 5)
                ]
                a2 = [
                    (f[q] + (a1[q - 2] + a1[q] + flat_sum(a1[q - 1]))) * r[q - 2]
                    for q in range(2, 4)
                ]
            for k in range(2):
                turn[pl.ds(k * ROWS * PART + n, ROWS, stride=PART), :] = a2[k]
            return carry

        lax.fori_loop(0, PART, one, 0, unroll=UNROLL)

    def pack(c):
        for k in range(2):
            for yy in range(ROWS):
                owner = (yy % 8) // 2
                rho = k * 4 + (yy // 8) * 2 + yy % 2
                at = (k * ROWS + yy) * PART
                outbox[c, owner, rho] = turn[at : at + PART, :].astype(BF16)

    def post(c, dz, dx):
        part = c % 2
        to_x = (x + dx) % 4
        if c < 2:
            dst = dirbox.at[p, part]
            target = dev(s, ((zh + dz) % 2) * 4 + to_x)
        else:
            dst = adjbox.at[x, h, part]
            target = dev(2 * j + (h + dz) % 2, zh * 4 + to_x)
        src = outbox.at[c, to_x]
        if dz == 0 and dx == 0:
            return pltpu.make_async_copy(src, dst, post_r.at[c, 0])
        return pltpu.make_async_remote_copy(
            src_ref=src,
            dst_ref=dst,
            send_sem=post_s.at[c, dz * 4 + dx],
            recv_sem=post_r.at[c, dz * 4 + dx],
            device_id=target,
            device_id_type=MESH,
        )

    def post_arrival(c, dz, dx):
        part = c % 2
        from_x = (x + 4 - dx) % 4
        if c < 2:
            dst = dirbox.at[((zh + dz) % 2) * 4 + from_x, part]
        else:
            dst = adjbox.at[from_x, (h + dz) % 2, part]
        pltpu.make_async_remote_copy(
            src_ref=outbox.at[c, 0],
            dst_ref=dst,
            send_sem=post_s.at[c, 0],
            recv_sem=post_r.at[c, dz * 4 + dx],
            device_id=dev(s, p),
            device_id_type=MESH,
        ).wait_recv()

    far_first = [(dz, dx) for dz in (1, 0) for dx in (2, 1, 3, 0)]
    for c in range(4):
        halo_own(c).wait()
        from_neighbours(halo_arrival(c))
        smooth(c // 2, c % 2)
        pack(c)
        for dz, dx in far_first:
            post(c, dz, dx).start()

    lcopy.wait()
    rcopy.wait()
    inv_root = jnp.broadcast_to(1.0 / jnp.sqrt(sing[...]), (64, 64))
    across = lax.broadcasted_iota(jnp.int32, (64, 64), 1)
    along = lax.broadcasted_iota(jnp.int32, (64, 64), 0)
    inv_root = jnp.sum(jnp.where(across == along, inv_root, 0.0), axis=1, keepdims=True)
    left_s = (lbuf[...] * inv_root).astype(BF16)
    scaled = rbuf[...] * inv_root
    scaled = jnp.where(h == 1, pltpu.roll(scaled, 1024 - PART, 1), scaled)
    for zz in range(2):
        rscaled[zz] = jnp.concatenate(
            [scaled[:, q * 64 : q * 64 + PART] for q in range(zz * 8, zz * 8 + 8)], axis=1
        ).astype(BF16)

    def arrived(c, dz):
        for dx in (2, 1, 3, 0):
            if dz == 0 and dx == 0:
                post(c, 0, 0).wait()
            else:
                post_arrival(c, dz, dx)

    def adj_rows(dx):
        xx = (x + dx) % 4
        pieces = [
            jnp.concatenate([adjbox[xx, hh, part, rho] for rho in range(8)], axis=1)
            for hh in range(2)
            for part in range(2)
        ]
        return jnp.concatenate(pieces, axis=0)

    def dir_rows(zz, yy, part):
        pieces = [
            jnp.concatenate(
                [dirbox[4 * zz + 2 * t + yy // 2, part, rho] for rho in range(8)], axis=1
            )
            for t in range(2)
        ]
        return jnp.concatenate(pieces, axis=0)

    def sa_copy(half, dy, dx):
        return pltpu.make_async_remote_copy(
            src_ref=psend.at[half, dy * 4 + dx],
            dst_ref=precv.at[half, dy * 4 + dx],
            send_sem=sa_s.at[half, dy * 4 + dx],
            recv_sem=sa_r.at[half, dy * 4 + dx],
            device_id=dev(2 * (zl * 4 + (y + dy) % 4) + h, zh * 4 + (x + dx) % 4),
            device_id_type=MESH,
        )

    def ship(half, dy, dx, block):
        psend[half, dy * 4 + dx] = block.astype(BF16)
        sa_copy(half, dy, dx).start()

    arrived(0, 0)
    arrived(1, 0)
    arrived(2, 1)
    arrived(2, 0)
    arrived(3, 1)
    arrived(3, 0)
    turns = (2, 1, 3, 0)
    dir_own = jnp.concatenate(
        [dir_rows(zh, (y + dy) % 4, (y + dy) % 2) for dy in turns], axis=0
    )
    for dx in turns:
        block = contract_last(dir_own, adj_rows(dx))
        for i, dy in enumerate(turns):
            if dx == 0 and dy == 0:
                gsum[0] = block[64 * i : 64 * i + 64]
            else:
                ship(0, dy, dx, block[64 * i : 64 * i + 64])

    def dir_cells(zz, k, t):
        rho = k * 4 + 2 * zh + t
        return jnp.concatenate(
            [dirbox[4 * zz + i, part, rho] for i in range(4) for part in range(2)], axis=0
        )

    def adj_cells(zz, t):
        rho = h * 4 + 2 * zz + t
        return jnp.concatenate(
            [adjbox[xx, hh, part, rho] for xx in range(4) for hh in range(2) for part in range(2)],
            axis=0,
        )

    def md_copy(fam):
        target = dev(2 * j + 1 - h, p) if fam == 0 else dev(s, (1 - zh) * 4 + x)
        return pltpu.make_async_remote_copy(
            src_ref=mpart.at[fam],
            dst_ref=mrecv.at[fam],
            send_sem=md_s.at[fam],
            recv_sem=md_r.at[fam],
            device_id=target,
            device_id_type=MESH,
        )

    for t in range(2):
        mpart[1, t] = product(left_s, adj_cells(1 - zh, t))
    md_copy(1).start()
    for t in range(2):
        mpart[0, t] = product(rscaled[zh], dir_cells(zh, 1 - h, t))
        dm_o[:, t, :] = product(rscaled[zh], dir_cells(zh, h, t))
        am_o[:, t, :] = product(left_s, adj_cells(zh, t))

    def other_half(part):
        first = dir_rows(1 - zh, part, part)
        second = dir_rows(1 - zh, 2 + part, part)
        rows = jnp.concatenate([first, second], axis=0)
        for dx in turns:
            block = contract_last(rows, adj_rows(dx))
            for i in range(2):
                piece = block[64 * i : 64 * i + 64]
                dy = (2 * i + part - y + 4) % 4
                if dx:
                    ship(1, dy, dx, piece)
                else:
                    @pl.when(dy == 0)
                    def _():
                        gsum[1] = piece

                    @pl.when(dy != 0)
                    def _():
                        ship(1, dy, dx, piece)

    def sb_copy(dz):
        return pltpu.make_async_remote_copy(
            src_ref=bsend.at[(zl + dz) % 4],
            dst_ref=brecv.at[dz],
            send_sem=sb_s.at[dz],
            recv_sem=sb_r.at[dz],
            device_id=dev(2 * (((zl + dz) % 4) * 4 + y) + h, p),
            device_id_type=MESH,
        )

    def add_up(half):
        for dy in (1, 3, 2, 0):
            for dx in (1, 3, 2, 0):
                if dy or dx:
                    sa_copy(half, dy, dx).wait_recv()
        total = gsum[half]
        for i in range(1, 16):
            total = total + precv[half, i].astype(F32)
        zz = zh if half == 0 else 1 - zh
        for t in range(2):
            bsend[2 * zz + t] = total[t * 32 : t * 32 + 32]
        for dz in (2, 1, 3):
            @pl.when(((zl + dz) % 4) // 2 == zz)
            def _():
                sb_copy(dz).start()

    arrived(0, 1)
    other_half(0)
    add_up(0)
    arrived(1, 1)
    other_half(1)
    for t in range(2):
        mpart[0, t] = mpart[0, t] + product(rscaled[1 - zh], dir_cells(1 - zh, 1 - h, t))
    md_copy(0).start()
    for t in range(2):
        dm_o[:, t, :] = dm_o[:, t, :] + product(rscaled[1 - zh], dir_cells(1 - zh, h, t))
    md_copy(1).wait_recv()
    for t in range(2):
        am_o[:, t, :] = am_o[:, t, :] + mrecv[1, t]
    add_up(1)
    md_copy(0).wait_recv()
    for t in range(2):
        dm_o[:, t, :] = dm_o[:, t, :] + mrecv[0, t]
    for dz in (1, 3, 2):
        sb_copy(dz).wait_recv()
    gram_o[...] = (bsend[zl] + brecv[1] + brecv[2] + brecv[3]) * weight

    to_neighbours(lambda dj, half: cond_copy(dj, half).wait_send())
    for c in range(4):
        to_neighbours(lambda dj, half: halo_copy(c, dj, half).wait_send())
        for dz, dx in far_first:
            if dz or dx:
                post(c, dz, dx).wait_send()
    for dy in range(4):
        for dx in range(4):
            if dy or dx:
                sa_copy(0, dy, dx).wait_send()
                sa_copy(1, dy, dx).wait_send()
    for dz in range(1, 4):
        sb_copy(dz).wait_send()
    for fam in range(2):
        md_copy(fam).wait_send()


def per_device(
    forcing_direct,
    forcing_adjoint,
    conductance,
    shift_table,
    freq_direct,
    freq_adjoint,
    left_factors,
    right_factors,
    singular_values,
):
    hold = lambda v: pltpu.with_memory_space_constraint(v, pltpu.HBM)
    weight = 1.0 / math.sqrt(32 * ROWS * LANES)
    any_ = pl.BlockSpec(memory_space=pltpu.HBM)
    vmem = pl.BlockSpec(memory_space=pltpu.VMEM)
    smem = pl.BlockSpec(memory_space=pltpu.SMEM)
    dma = pltpu.SemaphoreType.DMA
    gram, direct_modes, adjoint_modes = pl.pallas_call(
        functools.partial(kernel, weight),
        out_shape=(
            jax.ShapeDtypeStruct((32, 128), F32),
            jax.ShapeDtypeStruct((64, 2, LANES), F32),
            jax.ShapeDtypeStruct((64, 2, LANES), F32),
        ),
        in_specs=[any_, any_, any_, smem, smem, smem, any_, any_, vmem],
        out_specs=(vmem, vmem, vmem),
        scratch_shapes=[
            pltpu.VMEM((2, 2, PLANES, PART, ROWS, LANES), BF16),
            pltpu.VMEM((PLANES, ROWS, LANES), F32),
            pltpu.VMEM((LEVELS, PLANES, ROWS, LANES), F32),
            pltpu.VMEM((LEVELS, PLANES, ROWS, LANES), F32),
            pltpu.VMEM((2 * ROWS * PART, LANES), F32),
            pltpu.VMEM((4, 4, 8, PART, LANES), BF16),
            pltpu.VMEM((8, 2, 8, PART, LANES), BF16),
            pltpu.VMEM((4, 2, 2, 8, PART, LANES), BF16),
            pltpu.VMEM((2, 16, 64, 128), BF16),
            pltpu.VMEM((2, 16, 64, 128), BF16),
            pltpu.VMEM((2, 64, 128), F32),
            pltpu.VMEM((4, 32, 128), F32),
            pltpu.VMEM((4, 32, 128), F32),
            pltpu.VMEM((2, 2, 64, LANES), F32),
            pltpu.VMEM((2, 2, 64, LANES), F32),
            pltpu.VMEM((64, 512), F32),
            pltpu.VMEM((64, 1024), F32),
            pltpu.VMEM((2, 64, 256), BF16),
            dma((4, 6)), dma((4, 6)),
            dma((6,)), dma((6,)),
            dma((7,)),
            dma((4, 8)), dma((4, 8)),
            dma((2, 16)), dma((2, 16)),
            dma((4,)), dma((4,)),
            dma((2,)), dma((2,)),
        ],
        compiler_params=pltpu.CompilerParams(
            collective_id=0, has_side_effects=True, vmem_limit_bytes=50 * 1024 * 1024
        ),
        name="window",
    )(
        hold(forcing_direct.reshape(128, ROWS, LANES)),
        hold(forcing_adjoint.reshape(128, ROWS, LANES)),
        hold(conductance.reshape(ROWS, LANES)),
        hold(shift_table),
        hold(freq_direct),
        hold(freq_adjoint),
        hold(left_factors.T),
        hold(right_factors.T),
        hold(singular_values.reshape(1, 64)),
    )
    return (
        gram.T,
        direct_modes.reshape(64, 1, 2, LANES),
        adjoint_modes.reshape(64, 1, 2, LANES),
    )


def solution(mesh):
    placed = (
        P("snap", "space", None, None),
        P("snap", "space", None, None),
        P("space", None, None),
        P(),
        P("snap"),
        P("snap"),
        P(),
        P(),
        P(),
    )
    return jax.shard_map(
        per_device,
        mesh=mesh,
        in_specs=placed,
        out_specs=(
            P("snap", "space"),
            P(None, "space", "snap", None),
            P(None, "space", "snap", None),
        ),
        check_vma=False,
    )
```

```python
import functools
import math

import jax
import jax.numpy as jnp
from jax import lax
from jax.experimental import pallas as pl
from jax.experimental.pallas import tpu as pltpu
from jax.sharding import PartitionSpec as P

MESH = pl.DeviceIdType.MESH
F32 = jnp.float32
BF16 = jnp.bfloat16

ROWS = 16
LANES = 128
PLANES = 6
PART = 32
LEVELS = 16
UNROLL = 2


def contract_last(a, b):
    return lax.dot_general(a, b, (((1,), (1,)), ((), ())), preferred_element_type=F32)


def product(a, b):
    return lax.dot_general(a, b, (((1,), (0,)), ((), ())), preferred_element_type=F32)


def kernel(
    weight,
    fd, fa, cond, table, freq_d, freq_a, left, right, sing,
    gram_o, dm_o, am_o,
    field, chalo, rtab, crtab, turn, outbox, dirbox, adjbox,
    psend, precv, gsum, bsend, brecv, mpart, mrecv, lbuf, rbuf, rscaled,
    halo_s, halo_r, cond_s, cond_r, load_s, post_s, post_r, sa_s, sa_r, sb_s, sb_r, md_s, md_r,
):
    s = lax.axis_index("space")
    p = lax.axis_index("snap")
    j, h = s // 2, s % 2
    zl, y = j // 4, j % 4
    zh, x = p // 4, p % 4
    forcing = (fd, fa)

    def dev(ss, pp):
        return (ss, pp)

    barrier = pltpu.get_barrier_semaphore()
    greet = [dev(2 * j + 1 - h, p)]
    for dj in (-1, 1):
        for dh in (0, 1):
            greet.append(dev(2 * ((j + dj + 16) % 16) + dh, p))
    for dz in range(2):
        for dx in range(4):
            if dz or dx:
                greet.append(dev(s, ((zh + dz) % 2) * 4 + (x + dx) % 4))
    for dx in range(1, 4):
        greet.append(dev(2 * j + 1 - h, zh * 4 + (x + dx) % 4))
    for dy in range(1, 4):
        for dx in range(4):
            greet.append(dev(2 * (zl * 4 + (y + dy) % 4) + h, zh * 4 + (x + dx) % 4))
    for dz in range(1, 4):
        greet.append(dev(2 * (((zl + dz) % 4) * 4 + y) + h, p))
    for target in greet:
        pl.semaphore_signal(barrier, inc=1, device_id=target, device_id_type=MESH)
    pl.semaphore_wait(barrier, len(greet))

    def start_row(fam, part, half):
        return part * 64 + half * 32 if fam == 0 else half * 64 + part * 32

    def halo_copy(c, dj, half):
        fam, part = c // 2, c % 2
        slot = 2 * (dj + 1)
        return pltpu.make_async_remote_copy(
            src_ref=forcing[fam].at[pl.ds(start_row(fam, part, half), PART)],
            dst_ref=field.at[fam, part, 2 * (1 - dj) + h],
            send_sem=halo_s.at[c, slot + half],
            recv_sem=halo_r.at[c, 2 * (1 - dj) + h],
            device_id=dev(2 * (j + dj) + half, p),
            device_id_type=MESH,
        )

    def halo_own(c):
        fam, part = c // 2, c % 2
        return pltpu.make_async_copy(
            forcing[fam].at[pl.ds(start_row(fam, part, h), PART)],
            field.at[fam, part, 2 + h],
            load_s.at[c],
        )

    def cond_copy(dj, half):
        return pltpu.make_async_remote_copy(
            src_ref=cond,
            dst_ref=chalo.at[2 * (1 - dj) + h],
            send_sem=cond_s.at[2 * (dj + 1) + half],
            recv_sem=cond_r.at[2 * (1 - dj) + h],
            device_id=dev(2 * (j + dj) + half, p),
            device_id_type=MESH,
        )

    def to_neighbours(act):
        for dj, inside in ((1, j < 15), (-1, j > 0)):
            @pl.when(inside)
            def _():
                for half in range(2):
                    act(dj, half)
        act(0, 1 - h)

    def from_neighbours(act):
        for dj, inside in ((-1, j > 0), (1, j < 15)):
            @pl.when(inside)
            def _():
                for half in range(2):
                    act(dj, half)
        act(0, 1 - h)

    to_neighbours(lambda dj, half: cond_copy(dj, half).start())
    for c in range(4):
        to_neighbours(lambda dj, half: halo_copy(c, dj, half).start())
        halo_own(c).start()
    lcopy = pltpu.make_async_copy(left.at[:, pl.ds(pl.multiple_of(zh * 512, 512), 512)], lbuf, load_s.at[4])
    rcopy = pltpu.make_async_copy(right, rbuf, load_s.at[5])
    ccopy = pltpu.make_async_copy(cond, chalo.at[2 + h], load_s.at[6])
    lcopy.start()
    rcopy.start()
    ccopy.start()

    for first, edge in ((0, j == 0), (4, j == 15)):
        @pl.when(edge)
        def _():
            for k in range(2):
                chalo[first + k] = jnp.ones((ROWS, LANES), F32)
                for fam in range(2):
                    for part in range(2):
                        field[fam, part, first + k] = jnp.zeros((PART, ROWS, LANES), BF16)

    def cond_arrival(dj, half):
        pltpu.make_async_remote_copy(
            src_ref=cond,
            dst_ref=chalo.at[2 * (1 + dj) + half],
            send_sem=cond_s.at[0],
            recv_sem=cond_r.at[2 * (1 + dj) + half],
            device_id=dev(s, p),
            device_id_type=MESH,
        ).wait_recv()

    def halo_arrival(c):
        fam, part = c // 2, c % 2

        def act(dj, half):
            pltpu.make_async_remote_copy(
                src_ref=forcing[fam].at[pl.ds(0, PART)],
                dst_ref=field.at[fam, part, 2 * (1 + dj) + half],
                send_sem=halo_s.at[c, 0],
                recv_sem=halo_r.at[c, 2 * (1 + dj) + half],
                device_id=dev(s, p),
                device_id_type=MESH,
            ).wait_recv()

        return act

    ccopy.wait()
    from_neighbours(cond_arrival)

    def fill(level, carry):
        shift = table[level]
        for q in range(PLANES):
            there = j + (q // 2 - 1)
            mask = jnp.where((there >= 0) & (there < 16), F32(1.0), F32(0.0))
            coeff = chalo[q]
            inverse = mask / (shift + 6.0 * coeff)
            rtab[level, q] = inverse
            crtab[level, q] = coeff * inverse
        return carry

    lax.fori_loop(0, LEVELS, fill, 0)

    row = lax.broadcasted_iota(jnp.int32, (ROWS, LANES), 0)
    lane = lax.broadcasted_iota(jnp.int32, (ROWS, LANES), 1)

    def flat_sum(v):
        up = jnp.where(row == 0, 0.0, pltpu.roll(v, 1, 0))
        down = jnp.where(row == ROWS - 1, 0.0, pltpu.roll(v, ROWS - 1, 0))
        fore = jnp.where(lane == 0, 0.0, pltpu.roll(v, 1, 1))
        aft = jnp.where(lane == LANES - 1, 0.0, pltpu.roll(v, LANES - 1, 1))
        return (up + down) + (fore + aft)

    def smooth(fam, part):
        freq = freq_d if fam == 0 else freq_a
        base = start_row(fam, part, h)

        def one(n, carry):
            level = freq[base + n]
            f = [field[fam, part, q, n].astype(F32) for q in range(PLANES)]
            if fam == 0:
                r = [rtab[level, q] for q in range(PLANES)]
                g = [crtab[level, q] for q in range(1, 5)]
                a0 = [f[q] * r[q] for q in range(PLANES)]
                a1 = [
                    a0[q] + g[q - 1] * (a0[q - 1] + a0[q + 1] + flat_sum(a0[q]))
                    for q in range(1, 5)
                ]
                a2 = [
                    a0[q] + g[q - 1] * (a1[q - 2] + a1[q] + flat_sum(a1[q - 1]))
                    for q in range(2, 4)
                ]
            else:
                g = [crtab[level, q] for q in range(PLANES)]
                r = [rtab[level, q] for q in range(2, 4)]
                a0 = [f[q] * g[q] for q in range(PLANES)]
                a1 = [
                    a0[q] + g[q] * (a0[q - 1] + a0[q + 1] + flat_sum(a0[q]))
                    for q in range(1, 5)
                ]
                a2 = [
                    (f[q] + (a1[q - 2] + a1[q] + flat_sum(a1[q - 1]))) * r[q - 2]
                    for q in range(2, 4)
                ]
            for k in range(2):
                turn[pl.ds(k * ROWS * PART + n, ROWS, stride=PART), :] = a2[k]
            return carry

        lax.fori_loop(0, PART, one, 0, unroll=UNROLL)

    def pack(c):
        for k in range(2):
            for yy in range(ROWS):
                owner = (yy % 8) // 2
                rho = k * 4 + (yy // 8) * 2 + yy % 2
                at = (k * ROWS + yy) * PART
                outbox[c, owner, rho] = turn[at : at + PART, :].astype(BF16)

    def post(c, dz, dx):
        part = c % 2
        to_x = (x + dx) % 4
        if c < 2:
            dst = dirbox.at[p, part]
            target = dev(s, ((zh + dz) % 2) * 4 + to_x)
        else:
            dst = adjbox.at[x, h, part]
            target = dev(2 * j + (h + dz) % 2, zh * 4 + to_x)
        src = outbox.at[c, to_x]
        if dz == 0 and dx == 0:
            return pltpu.make_async_copy(src, dst, post_r.at[c, 0])
        return pltpu.make_async_remote_copy(
            src_ref=src,
            dst_ref=dst,
            send_sem=post_s.at[c, dz * 4 + dx],
            recv_sem=post_r.at[c, dz * 4 + dx],
            device_id=target,
            device_id_type=MESH,
        )

    def post_arrival(c, dz, dx):
        part = c % 2
        from_x = (x + 4 - dx) % 4
        if c < 2:
            dst = dirbox.at[((zh + dz) % 2) * 4 + from_x, part]
        else:
            dst = adjbox.at[from_x, (h + dz) % 2, part]
        pltpu.make_async_remote_copy(
            src_ref=outbox.at[c, 0],
            dst_ref=dst,
            send_sem=post_s.at[c, 0],
            recv_sem=post_r.at[c, dz * 4 + dx],
            device_id=dev(s, p),
            device_id_type=MESH,
        ).wait_recv()

    far_first = [(dz, dx) for dz in (1, 0) for dx in (3, 2, 1, 0)]
    for c in range(4):
        halo_own(c).wait()
        from_neighbours(halo_arrival(c))
        smooth(c // 2, c % 2)
        pack(c)
        for dz, dx in far_first:
            post(c, dz, dx).start()

    lcopy.wait()
    rcopy.wait()
    inv_root = jnp.broadcast_to(1.0 / jnp.sqrt(sing[...]), (64, 64))
    across = lax.broadcasted_iota(jnp.int32, (64, 64), 1)
    along = lax.broadcasted_iota(jnp.int32, (64, 64), 0)
    inv_root = jnp.sum(jnp.where(across == along, inv_root, 0.0), axis=1, keepdims=True)
    left_s = (lbuf[...] * inv_root).astype(BF16)
    scaled = rbuf[...] * inv_root
    scaled = jnp.where(h == 1, pltpu.roll(scaled, 1024 - PART, 1), scaled)
    for zz in range(2):
        rscaled[zz] = jnp.concatenate(
            [scaled[:, q * 64 : q * 64 + PART] for q in range(zz * 8, zz * 8 + 8)], axis=1
        ).astype(BF16)

    def arrived(c, dz):
        for dx in (2, 1, 3, 0):
            if dz == 0 and dx == 0:
                post(c, 0, 0).wait()
            else:
                post_arrival(c, dz, dx)

    def adj_rows(dx):
        xx = (x + dx) % 4
        pieces = [
            jnp.concatenate([adjbox[xx, hh, part, rho] for rho in range(8)], axis=1)
            for hh in range(2)
            for part in range(2)
        ]
        return jnp.concatenate(pieces, axis=0)

    def dir_rows(zz, yy, part):
        pieces = [
            jnp.concatenate(
                [dirbox[4 * zz + 2 * t + yy // 2, part, rho] for rho in range(8)], axis=1
            )
            for t in range(2)
        ]
        return jnp.concatenate(pieces, axis=0)

    def sa_copy(half, dy, dx):
        return pltpu.make_async_remote_copy(
            src_ref=psend.at[half, dy * 4 + dx],
            dst_ref=precv.at[half, dy * 4 + dx],
            send_sem=sa_s.at[half, dy * 4 + dx],
            recv_sem=sa_r.at[half, dy * 4 + dx],
            device_id=dev(2 * (zl * 4 + (y + dy) % 4) + h, zh * 4 + (x + dx) % 4),
            device_id_type=MESH,
        )

    def ship(half, dy, dx, block):
        psend[half, dy * 4 + dx] = block.astype(BF16)
        sa_copy(half, dy, dx).start()

    arrived(0, 0)
    arrived(1, 0)
    arrived(2, 1)
    arrived(2, 0)
    arrived(3, 1)
    arrived(3, 0)
    turns = (2, 1, 3, 0)
    dir_own = jnp.concatenate(
        [dir_rows(zh, (y + dy) % 4, (y + dy) % 2) for dy in turns], axis=0
    )
    for dx in turns:
        block = contract_last(dir_own, adj_rows(dx))
        for i, dy in enumerate(turns):
            if dx == 0 and dy == 0:
                gsum[0] = block[64 * i : 64 * i + 64]
            else:
                ship(0, dy, dx, block[64 * i : 64 * i + 64])

    def dir_cells(zz, k, t):
        rho = k * 4 + 2 * zh + t
        return jnp.concatenate(
            [dirbox[4 * zz + i, part, rho] for i in range(4) for part in range(2)], axis=0
        )

    def adj_cells(zz, t):
        rho = h * 4 + 2 * zz + t
        return jnp.concatenate(
            [adjbox[xx, hh, part, rho] for xx in range(4) for hh in range(2) for part in range(2)],
            axis=0,
        )

    def md_copy(fam):
        target = dev(2 * j + 1 - h, p) if fam == 0 else dev(s, (1 - zh) * 4 + x)
        return pltpu.make_async_remote_copy(
            src_ref=mpart.at[fam],
            dst_ref=mrecv.at[fam],
            send_sem=md_s.at[fam],
            recv_sem=md_r.at[fam],
            device_id=target,
            device_id_type=MESH,
        )

    for t in range(2):
        mpart[1, t] = product(left_s, adj_cells(1 - zh, t))
    md_copy(1).start()
    for t in range(2):
        mpart[0, t] = product(rscaled[zh], dir_cells(zh, 1 - h, t))
        dm_o[:, t, :] = product(rscaled[zh], dir_cells(zh, h, t))
        am_o[:, t, :] = product(left_s, adj_cells(zh, t))

    def other_half(part):
        first = dir_rows(1 - zh, part, part)
        second = dir_rows(1 - zh, 2 + part, part)
        rows = jnp.concatenate([first, second], axis=0)
        for dx in turns:
            block = contract_last(rows, adj_rows(dx))
            for i in range(2):
                piece = block[64 * i : 64 * i + 64]
                dy = (2 * i + part - y + 4) % 4
                if dx:
                    ship(1, dy, dx, piece)
                else:
                    @pl.when(dy == 0)
                    def _():
                        gsum[1] = piece

                    @pl.when(dy != 0)
                    def _():
                        ship(1, dy, dx, piece)

    def sb_copy(dz):
        return pltpu.make_async_remote_copy(
            src_ref=bsend.at[(zl + dz) % 4],
            dst_ref=brecv.at[dz],
            send_sem=sb_s.at[dz],
            recv_sem=sb_r.at[dz],
            device_id=dev(2 * (((zl + dz) % 4) * 4 + y) + h, p),
            device_id_type=MESH,
        )

    def add_up(half):
        for dy in (1, 3, 2, 0):
            for dx in (1, 3, 2, 0):
                if dy or dx:
                    sa_copy(half, dy, dx).wait_recv()
        total = gsum[half]
        for i in range(1, 16):
            total = total + precv[half, i].astype(F32)
        zz = zh if half == 0 else 1 - zh
        for t in range(2):
            bsend[2 * zz + t] = total[t * 32 : t * 32 + 32]
        for dz in (2, 1, 3):
            @pl.when(((zl + dz) % 4) // 2 == zz)
            def _():
                sb_copy(dz).start()

    arrived(0, 1)
    other_half(0)
    add_up(0)
    arrived(1, 1)
    other_half(1)
    for t in range(2):
        mpart[0, t] = mpart[0, t] + product(rscaled[1 - zh], dir_cells(1 - zh, 1 - h, t))
    md_copy(0).start()
    for t in range(2):
        dm_o[:, t, :] = dm_o[:, t, :] + product(rscaled[1 - zh], dir_cells(1 - zh, h, t))
    md_copy(1).wait_recv()
    for t in range(2):
        am_o[:, t, :] = am_o[:, t, :] + mrecv[1, t]
    add_up(1)
    md_copy(0).wait_recv()
    for t in range(2):
        dm_o[:, t, :] = dm_o[:, t, :] + mrecv[0, t]
    for dz in (1, 3, 2):
        sb_copy(dz).wait_recv()
    gram_o[...] = (bsend[zl] + brecv[1] + brecv[2] + brecv[3]) * weight

    to_neighbours(lambda dj, half: cond_copy(dj, half).wait_send())
    for c in range(4):
        to_neighbours(lambda dj, half: halo_copy(c, dj, half).wait_send())
        for dz, dx in far_first:
            if dz or dx:
                post(c, dz, dx).wait_send()
    for dy in range(4):
        for dx in range(4):
            if dy or dx:
                sa_copy(0, dy, dx).wait_send()
                sa_copy(1, dy, dx).wait_send()
    for dz in range(1, 4):
        sb_copy(dz).wait_send()
    for fam in range(2):
        md_copy(fam).wait_send()


def per_device(
    forcing_direct,
    forcing_adjoint,
    conductance,
    shift_table,
    freq_direct,
    freq_adjoint,
    left_factors,
    right_factors,
    singular_values,
):
    hold = lambda v: pltpu.with_memory_space_constraint(v, pltpu.HBM)
    weight = 1.0 / math.sqrt(32 * ROWS * LANES)
    any_ = pl.BlockSpec(memory_space=pltpu.HBM)
    vmem = pl.BlockSpec(memory_space=pltpu.VMEM)
    smem = pl.BlockSpec(memory_space=pltpu.SMEM)
    dma = pltpu.SemaphoreType.DMA
    gram, direct_modes, adjoint_modes = pl.pallas_call(
        functools.partial(kernel, weight),
        out_shape=(
            jax.ShapeDtypeStruct((32, 128), F32),
            jax.ShapeDtypeStruct((64, 2, LANES), F32),
            jax.ShapeDtypeStruct((64, 2, LANES), F32),
        ),
        in_specs=[any_, any_, any_, smem, smem, smem, any_, any_, vmem],
        out_specs=(vmem, vmem, vmem),
        scratch_shapes=[
            pltpu.VMEM((2, 2, PLANES, PART, ROWS, LANES), BF16),
            pltpu.VMEM((PLANES, ROWS, LANES), F32),
            pltpu.VMEM((LEVELS, PLANES, ROWS, LANES), F32),
            pltpu.VMEM((LEVELS, PLANES, ROWS, LANES), F32),
            pltpu.VMEM((2 * ROWS * PART, LANES), F32),
            pltpu.VMEM((4, 4, 8, PART, LANES), BF16),
            pltpu.VMEM((8, 2, 8, PART, LANES), BF16),
            pltpu.VMEM((4, 2, 2, 8, PART, LANES), BF16),
            pltpu.VMEM((2, 16, 64, 128), BF16),
            pltpu.VMEM((2, 16, 64, 128), BF16),
            pltpu.VMEM((2, 64, 128), F32),
            pltpu.VMEM((4, 32, 128), F32),
            pltpu.VMEM((4, 32, 128), F32),
            pltpu.VMEM((2, 2, 64, LANES), F32),
            pltpu.VMEM((2, 2, 64, LANES), F32),
            pltpu.VMEM((64, 512), F32),
            pltpu.VMEM((64, 1024), F32),
            pltpu.VMEM((2, 64, 256), BF16),
            dma((4, 6)), dma((4, 6)),
            dma((6,)), dma((6,)),
            dma((7,)),
            dma((4, 8)), dma((4, 8)),
            dma((2, 16)), dma((2, 16)),
            dma((4,)), dma((4,)),
            dma((2,)), dma((2,)),
        ],
        compiler_params=pltpu.CompilerParams(
            collective_id=0, has_side_effects=True, vmem_limit_bytes=50 * 1024 * 1024
        ),
        name="window",
    )(
        hold(forcing_direct.reshape(128, ROWS, LANES)),
        hold(forcing_adjoint.reshape(128, ROWS, LANES)),
        hold(conductance.reshape(ROWS, LANES)),
        hold(shift_table),
        hold(freq_direct),
        hold(freq_adjoint),
        hold(left_factors.T),
        hold(right_factors.T),
        hold(singular_values.reshape(1, 64)),
    )
    return (
        gram.T,
        direct_modes.reshape(64, 1, 2, LANES),
        adjoint_modes.reshape(64, 1, 2, LANES),
    )


def solution(mesh):
    placed = (
        P("snap", "space", None, None),
        P("snap", "space", None, None),
        P("space", None, None),
        P(),
        P("snap"),
        P("snap"),
        P(),
        P(),
        P(),
    )
    return jax.shard_map(
        per_device,
        mesh=mesh,
        in_specs=placed,
        out_specs=(
            P("snap", "space"),
            P(None, "space", "snap", None),
            P(None, "space", "snap", None),
        ),
        check_vma=False,
    )
```

```python
import functools
import math

import jax
import jax.numpy as jnp
from jax import lax
from jax.experimental import pallas as pl
from jax.experimental.pallas import tpu as pltpu
from jax.sharding import PartitionSpec as P

MESH = pl.DeviceIdType.MESH
F32 = jnp.float32
BF16 = jnp.bfloat16

ROWS = 16
LANES = 128
PLANES = 6
PART = 32
LEVELS = 16
UNROLL = 2


def contract_last(a, b):
    return lax.dot_general(a, b, (((1,), (1,)), ((), ())), preferred_element_type=F32)


def product(a, b):
    return lax.dot_general(a, b, (((1,), (0,)), ((), ())), preferred_element_type=F32)


def kernel(
    weight,
    fd, fa, cond, table, freq_d, freq_a, left, right, sing,
    gram_o, dm_o, am_o,
    field, chalo, rtab, crtab, turn, outbox, dirbox, adjbox,
    psend, precv, gsum, bsend, brecv, mpart, mrecv, lbuf, rbuf, rscaled,
    halo_s, halo_r, cond_s, cond_r, load_s, post_s, post_r, sa_s, sa_r, sb_s, sb_r, md_s, md_r,
):
    s = lax.axis_index("space")
    p = lax.axis_index("snap")
    j, h = s // 2, s % 2
    zl, y = j // 4, j % 4
    zh, x = p // 4, p % 4
    forcing = (fd, fa)

    def dev(ss, pp):
        return (ss, pp)

    barrier = pltpu.get_barrier_semaphore()
    greet = [dev(2 * j + 1 - h, p)]
    for dj in (-1, 1):
        for dh in (0, 1):
            greet.append(dev(2 * ((j + dj + 16) % 16) + dh, p))
    for dz in range(2):
        for dx in range(4):
            if dz or dx:
                greet.append(dev(s, ((zh + dz) % 2) * 4 + (x + dx) % 4))
    for dx in range(1, 4):
        greet.append(dev(2 * j + 1 - h, zh * 4 + (x + dx) % 4))
    for dy in range(1, 4):
        for dx in range(4):
            greet.append(dev(2 * (zl * 4 + (y + dy) % 4) + h, zh * 4 + (x + dx) % 4))
    for dz in range(1, 4):
        greet.append(dev(2 * (((zl + dz) % 4) * 4 + y) + h, p))
    for target in greet:
        pl.semaphore_signal(barrier, inc=1, device_id=target, device_id_type=MESH)
    pl.semaphore_wait(barrier, len(greet))

    def start_row(fam, part, half):
        return part * 64 + half * 32 if fam == 0 else half * 64 + part * 32

    def halo_copy(c, dj, half):
        fam, part = c // 2, c % 2
        slot = 2 * (dj + 1)
        return pltpu.make_async_remote_copy(
            src_ref=forcing[fam].at[pl.ds(start_row(fam, part, half), PART)],
            dst_ref=field.at[fam, part, 2 * (1 - dj) + h],
            send_sem=halo_s.at[c, slot + half],
            recv_sem=halo_r.at[c, 2 * (1 - dj) + h],
            device_id=dev(2 * (j + dj) + half, p),
            device_id_type=MESH,
        )

    def halo_own(c):
        fam, part = c // 2, c % 2
        return pltpu.make_async_copy(
            forcing[fam].at[pl.ds(start_row(fam, part, h), PART)],
            field.at[fam, part, 2 + h],
            load_s.at[c],
        )

    def cond_copy(dj, half):
        return pltpu.make_async_remote_copy(
            src_ref=cond,
            dst_ref=chalo.at[2 * (1 - dj) + h],
            send_sem=cond_s.at[2 * (dj + 1) + half],
            recv_sem=cond_r.at[2 * (1 - dj) + h],
            device_id=dev(2 * (j + dj) + half, p),
            device_id_type=MESH,
        )

    def to_neighbours(act):
        for dj, inside in ((1, j < 15), (-1, j > 0)):
            @pl.when(inside)
            def _():
                for half in range(2):
                    act(dj, half)
        act(0, 1 - h)

    def from_neighbours(act):
        for dj, inside in ((-1, j > 0), (1, j < 15)):
            @pl.when(inside)
            def _():
                for half in range(2):
                    act(dj, half)
        act(0, 1 - h)

    to_neighbours(lambda dj, half: cond_copy(dj, half).start())
    for c in range(4):
        to_neighbours(lambda dj, half: halo_copy(c, dj, half).start())
        halo_own(c).start()
    lcopy = pltpu.make_async_copy(left.at[:, pl.ds(pl.multiple_of(zh * 512, 512), 512)], lbuf, load_s.at[4])
    rcopy = pltpu.make_async_copy(right, rbuf, load_s.at[5])
    ccopy = pltpu.make_async_copy(cond, chalo.at[2 + h], load_s.at[6])
    lcopy.start()
    rcopy.start()
    ccopy.start()

    for first, edge in ((0, j == 0), (4, j == 15)):
        @pl.when(edge)
        def _():
            for k in range(2):
                chalo[first + k] = jnp.ones((ROWS, LANES), F32)
                for fam in range(2):
                    for part in range(2):
                        field[fam, part, first + k] = jnp.zeros((PART, ROWS, LANES), BF16)

    def cond_arrival(dj, half):
        pltpu.make_async_remote_copy(
            src_ref=cond,
            dst_ref=chalo.at[2 * (1 + dj) + half],
            send_sem=cond_s.at[0],
            recv_sem=cond_r.at[2 * (1 + dj) + half],
            device_id=dev(s, p),
            device_id_type=MESH,
        ).wait_recv()

    def halo_arrival(c):
        fam, part = c // 2, c % 2

        def act(dj, half):
            pltpu.make_async_remote_copy(
                src_ref=forcing[fam].at[pl.ds(0, PART)],
                dst_ref=field.at[fam, part, 2 * (1 + dj) + half],
                send_sem=halo_s.at[c, 0],
                recv_sem=halo_r.at[c, 2 * (1 + dj) + half],
                device_id=dev(s, p),
                device_id_type=MESH,
            ).wait_recv()

        return act

    ccopy.wait()
    from_neighbours(cond_arrival)

    def fill(level, carry):
        shift = table[level]
        for q in range(PLANES):
            there = j + (q // 2 - 1)
            mask = jnp.where((there >= 0) & (there < 16), F32(1.0), F32(0.0))
            coeff = chalo[q]
            inverse = mask / (shift + 6.0 * coeff)
            rtab[level, q] = inverse
            crtab[level, q] = coeff * inverse
        return carry

    lax.fori_loop(0, LEVELS, fill, 0)

    row = lax.broadcasted_iota(jnp.int32, (ROWS, LANES), 0)
    lane = lax.broadcasted_iota(jnp.int32, (ROWS, LANES), 1)

    def flat_sum(v):
        up = jnp.where(row == 0, 0.0, pltpu.roll(v, 1, 0))
        down = jnp.where(row == ROWS - 1, 0.0, pltpu.roll(v, ROWS - 1, 0))
        fore = jnp.where(lane == 0, 0.0, pltpu.roll(v, 1, 1))
        aft = jnp.where(lane == LANES - 1, 0.0, pltpu.roll(v, LANES - 1, 1))
        return (up + down) + (fore + aft)

    def smooth(fam, part):
        freq = freq_d if fam == 0 else freq_a
        base = start_row(fam, part, h)

        def one(n, carry):
            level = freq[base + n]
            f = [field[fam, part, q, n].astype(F32) for q in range(PLANES)]
            if fam == 0:
                r = [rtab[level, q] for q in range(PLANES)]
                g = [crtab[level, q] for q in range(1, 5)]
                a0 = [f[q] * r[q] for q in range(PLANES)]
                a1 = [
                    a0[q] + g[q - 1] * (a0[q - 1] + a0[q + 1] + flat_sum(a0[q]))
                    for q in range(1, 5)
                ]
                a2 = [
                    a0[q] + g[q - 1] * (a1[q - 2] + a1[q] + flat_sum(a1[q - 1]))
                    for q in range(2, 4)
                ]
            else:
                g = [crtab[level, q] for q in range(PLANES)]
                r = [rtab[level, q] for q in range(2, 4)]
                a0 = [f[q] * g[q] for q in range(PLANES)]
                a1 = [
                    a0[q] + g[q] * (a0[q - 1] + a0[q + 1] + flat_sum(a0[q]))
                    for q in range(1, 5)
                ]
                a2 = [
                    (f[q] + (a1[q - 2] + a1[q] + flat_sum(a1[q - 1]))) * r[q - 2]
                    for q in range(2, 4)
                ]
            for k in range(2):
                turn[pl.ds(k * ROWS * PART + n, ROWS, stride=PART), :] = a2[k]
            return carry

        lax.fori_loop(0, PART, one, 0, unroll=UNROLL)

    def pack(c):
        for k in range(2):
            for yy in range(ROWS):
                owner = (yy % 8) // 2
                rho = k * 4 + (yy // 8) * 2 + yy % 2
                at = (k * ROWS + yy) * PART
                outbox[c, owner, rho] = turn[at : at + PART, :].astype(BF16)

    def post(c, dz, dx):
        part = c % 2
        to_x = (x + dx) % 4
        if c < 2:
            dst = dirbox.at[p, part]
            target = dev(s, ((zh + dz) % 2) * 4 + to_x)
        else:
            dst = adjbox.at[x, h, part]
            target = dev(2 * j + (h + dz) % 2, zh * 4 + to_x)
        src = outbox.at[c, to_x]
        if dz == 0 and dx == 0:
            return pltpu.make_async_copy(src, dst, post_r.at[c, 0])
        return pltpu.make_async_remote_copy(
            src_ref=src,
            dst_ref=dst,
            send_sem=post_s.at[c, dz * 4 + dx],
            recv_sem=post_r.at[c, dz * 4 + dx],
            device_id=target,
            device_id_type=MESH,
        )

    def post_arrival(c, dz, dx):
        part = c % 2
        from_x = (x + 4 - dx) % 4
        if c < 2:
            dst = dirbox.at[((zh + dz) % 2) * 4 + from_x, part]
        else:
            dst = adjbox.at[from_x, (h + dz) % 2, part]
        pltpu.make_async_remote_copy(
            src_ref=outbox.at[c, 0],
            dst_ref=dst,
            send_sem=post_s.at[c, 0],
            recv_sem=post_r.at[c, dz * 4 + dx],
            device_id=dev(s, p),
            device_id_type=MESH,
        ).wait_recv()

    far_first = [(dz, dx) for dz in (1, 0) for dx in (3, 2, 1, 0)]
    for c in range(4):
        halo_own(c).wait()
        from_neighbours(halo_arrival(c))
        smooth(c // 2, c % 2)
        pack(c)
        for dz, dx in far_first:
            post(c, dz, dx).start()

    lcopy.wait()
    rcopy.wait()
    inv_root = jnp.broadcast_to(1.0 / jnp.sqrt(sing[...]), (64, 64))
    across = lax.broadcasted_iota(jnp.int32, (64, 64), 1)
    along = lax.broadcasted_iota(jnp.int32, (64, 64), 0)
    inv_root = jnp.sum(jnp.where(across == along, inv_root, 0.0), axis=1, keepdims=True)
    left_s = (lbuf[...] * inv_root).astype(BF16)
    scaled = rbuf[...] * inv_root
    scaled = jnp.where(h == 1, pltpu.roll(scaled, 1024 - PART, 1), scaled)
    for zz in range(2):
        rscaled[zz] = jnp.concatenate(
            [scaled[:, q * 64 : q * 64 + PART] for q in range(zz * 8, zz * 8 + 8)], axis=1
        ).astype(BF16)

    def arrived(c, dz):
        for dx in (2, 1, 3, 0):
            if dz == 0 and dx == 0:
                post(c, 0, 0).wait()
            else:
                post_arrival(c, dz, dx)

    def adj_rows(dx):
        xx = (x + dx) % 4
        pieces = [
            jnp.concatenate([adjbox[xx, hh, part, rho] for rho in range(8)], axis=1)
            for hh in range(2)
            for part in range(2)
        ]
        return jnp.concatenate(pieces, axis=0)

    def dir_rows(zz, yy, part):
        pieces = [
            jnp.concatenate(
                [dirbox[4 * zz + 2 * t + yy // 2, part, rho] for rho in range(8)], axis=1
            )
            for t in range(2)
        ]
        return jnp.concatenate(pieces, axis=0)

    def sa_copy(half, dy, dx):
        return pltpu.make_async_remote_copy(
            src_ref=psend.at[half, dy * 4 + dx],
            dst_ref=precv.at[half, dy * 4 + dx],
            send_sem=sa_s.at[half, dy * 4 + dx],
            recv_sem=sa_r.at[half, dy * 4 + dx],
            device_id=dev(2 * (zl * 4 + (y + dy) % 4) + h, zh * 4 + (x + dx) % 4),
            device_id_type=MESH,
        )

    def ship(half, dy, dx, block):
        psend[half, dy * 4 + dx] = block.astype(BF16)
        sa_copy(half, dy, dx).start()

    arrived(0, 0)
    arrived(1, 0)
    arrived(2, 1)
    arrived(2, 0)
    arrived(3, 1)
    arrived(3, 0)
    turns = (2, 1, 3, 0)
    dir_own = jnp.concatenate(
        [dir_rows(zh, (y + dy) % 4, (y + dy) % 2) for dy in turns], axis=0
    )
    for dx in turns:
        block = contract_last(dir_own, adj_rows(dx))
        for i, dy in enumerate(turns):
            if dx == 0 and dy == 0:
                gsum[0] = block[64 * i : 64 * i + 64]
            else:
                ship(0, dy, dx, block[64 * i : 64 * i + 64])

    def dir_cells(zz, k, t):
        rho = k * 4 + 2 * zh + t
        return jnp.concatenate(
            [dirbox[4 * zz + i, part, rho] for i in range(4) for part in range(2)], axis=0
        )

    def adj_cells(zz, t):
        rho = h * 4 + 2 * zz + t
        return jnp.concatenate(
            [adjbox[xx, hh, part, rho] for xx in range(4) for hh in range(2) for part in range(2)],
            axis=0,
        )

    def md_copy(fam):
        target = dev(2 * j + 1 - h, p) if fam == 0 else dev(s, (1 - zh) * 4 + x)
        return pltpu.make_async_remote_copy(
            src_ref=mpart.at[fam],
            dst_ref=mrecv.at[fam],
            send_sem=md_s.at[fam],
            recv_sem=md_r.at[fam],
            device_id=target,
            device_id_type=MESH,
        )

    for t in range(2):
        mpart[1, t] = product(left_s, adj_cells(1 - zh, t))
    md_copy(1).start()
    for t in range(2):
        mpart[0, t] = product(rscaled[zh], dir_cells(zh, 1 - h, t))
        dm_o[:, t, :] = product(rscaled[zh], dir_cells(zh, h, t))
        am_o[:, t, :] = product(left_s, adj_cells(zh, t))

    def other_half(part):
        first = dir_rows(1 - zh, part, part)
        second = dir_rows(1 - zh, 2 + part, part)
        rows = jnp.concatenate([first, second], axis=0)
        for dx in turns:
            block = contract_last(rows, adj_rows(dx))
            for i in range(2):
                piece = block[64 * i : 64 * i + 64]
                dy = (2 * i + part - y + 4) % 4
                if dx:
                    ship(1, dy, dx, piece)
                else:
                    @pl.when(dy == 0)
                    def _():
                        gsum[1] = piece

                    @pl.when(dy != 0)
                    def _():
                        ship(1, dy, dx, piece)

    def sb_copy(dz):
        return pltpu.make_async_remote_copy(
            src_ref=bsend.at[(zl + dz) % 4],
            dst_ref=brecv.at[dz],
            send_sem=sb_s.at[dz],
            recv_sem=sb_r.at[dz],
            device_id=dev(2 * (((zl + dz) % 4) * 4 + y) + h, p),
            device_id_type=MESH,
        )

    def add_up(half):
        for dy in (1, 3, 2, 0):
            for dx in (1, 3, 2, 0):
                if dy or dx:
                    sa_copy(half, dy, dx).wait_recv()
        total = gsum[half]
        for i in range(1, 16):
            total = total + precv[half, i].astype(F32)
        zz = zh if half == 0 else 1 - zh
        for t in range(2):
            bsend[2 * zz + t] = total[t * 32 : t * 32 + 32]
        for dz in (2, 1, 3):
            @pl.when(((zl + dz) % 4) // 2 == zz)
            def _():
                sb_copy(dz).start()

    add_up(0)
    arrived(0, 1)
    other_half(0)
    arrived(1, 1)
    other_half(1)
    for t in range(2):
        mpart[0, t] = mpart[0, t] + product(rscaled[1 - zh], dir_cells(1 - zh, 1 - h, t))
    md_copy(0).start()
    for t in range(2):
        dm_o[:, t, :] = dm_o[:, t, :] + product(rscaled[1 - zh], dir_cells(1 - zh, h, t))
    md_copy(1).wait_recv()
    for t in range(2):
        am_o[:, t, :] = am_o[:, t, :] + mrecv[1, t]
    add_up(1)
    md_copy(0).wait_recv()
    for t in range(2):
        dm_o[:, t, :] = dm_o[:, t, :] + mrecv[0, t]
    for dz in (1, 3, 2):
        sb_copy(dz).wait_recv()
    gram_o[...] = (bsend[zl] + brecv[1] + brecv[2] + brecv[3]) * weight

    to_neighbours(lambda dj, half: cond_copy(dj, half).wait_send())
    for c in range(4):
        to_neighbours(lambda dj, half: halo_copy(c, dj, half).wait_send())
        for dz, dx in far_first:
            if dz or dx:
                post(c, dz, dx).wait_send()
    for dy in range(4):
        for dx in range(4):
            if dy or dx:
                sa_copy(0, dy, dx).wait_send()
                sa_copy(1, dy, dx).wait_send()
    for dz in range(1, 4):
        sb_copy(dz).wait_send()
    for fam in range(2):
        md_copy(fam).wait_send()


def per_device(
    forcing_direct,
    forcing_adjoint,
    conductance,
    shift_table,
    freq_direct,
    freq_adjoint,
    left_factors,
    right_factors,
    singular_values,
):
    hold = lambda v: pltpu.with_memory_space_constraint(v, pltpu.HBM)
    weight = 1.0 / math.sqrt(32 * ROWS * LANES)
    any_ = pl.BlockSpec(memory_space=pltpu.HBM)
    vmem = pl.BlockSpec(memory_space=pltpu.VMEM)
    smem = pl.BlockSpec(memory_space=pltpu.SMEM)
    dma = pltpu.SemaphoreType.DMA
    gram, direct_modes, adjoint_modes = pl.pallas_call(
        functools.partial(kernel, weight),
        out_shape=(
            jax.ShapeDtypeStruct((32, 128), F32),
            jax.ShapeDtypeStruct((64, 2, LANES), F32),
            jax.ShapeDtypeStruct((64, 2, LANES), F32),
        ),
        in_specs=[any_, any_, any_, smem, smem, smem, any_, any_, vmem],
        out_specs=(vmem, vmem, vmem),
        scratch_shapes=[
            pltpu.VMEM((2, 2, PLANES, PART, ROWS, LANES), BF16),
            pltpu.VMEM((PLANES, ROWS, LANES), F32),
            pltpu.VMEM((LEVELS, PLANES, ROWS, LANES), F32),
            pltpu.VMEM((LEVELS, PLANES, ROWS, LANES), F32),
            pltpu.VMEM((2 * ROWS * PART, LANES), F32),
            pltpu.VMEM((4, 4, 8, PART, LANES), BF16),
            pltpu.VMEM((8, 2, 8, PART, LANES), BF16),
            pltpu.VMEM((4, 2, 2, 8, PART, LANES), BF16),
            pltpu.VMEM((2, 16, 64, 128), BF16),
            pltpu.VMEM((2, 16, 64, 128), BF16),
            pltpu.VMEM((2, 64, 128), F32),
            pltpu.VMEM((4, 32, 128), F32),
            pltpu.VMEM((4, 32, 128), F32),
            pltpu.VMEM((2, 2, 64, LANES), F32),
            pltpu.VMEM((2, 2, 64, LANES), F32),
            pltpu.VMEM((64, 512), F32),
            pltpu.VMEM((64, 1024), F32),
            pltpu.VMEM((2, 64, 256), BF16),
            dma((4, 6)), dma((4, 6)),
            dma((6,)), dma((6,)),
            dma((7,)),
            dma((4, 8)), dma((4, 8)),
            dma((2, 16)), dma((2, 16)),
            dma((4,)), dma((4,)),
            dma((2,)), dma((2,)),
        ],
        compiler_params=pltpu.CompilerParams(
            collective_id=0, has_side_effects=True, vmem_limit_bytes=50 * 1024 * 1024
        ),
        name="window",
    )(
        hold(forcing_direct.reshape(128, ROWS, LANES)),
        hold(forcing_adjoint.reshape(128, ROWS, LANES)),
        hold(conductance.reshape(ROWS, LANES)),
        hold(shift_table),
        hold(freq_direct),
        hold(freq_adjoint),
        hold(left_factors.T),
        hold(right_factors.T),
        hold(singular_values.reshape(1, 64)),
    )
    return (
        gram.T,
        direct_modes.reshape(64, 1, 2, LANES),
        adjoint_modes.reshape(64, 1, 2, LANES),
    )


def solution(mesh):
    placed = (
        P("snap", "space", None, None),
        P("snap", "space", None, None),
        P("space", None, None),
        P(),
        P("snap"),
        P("snap"),
        P(),
        P(),
        P(),
    )
    return jax.shard_map(
        per_device,
        mesh=mesh,
        in_specs=placed,
        out_specs=(
            P("snap", "space"),
            P(None, "space", "snap", None),
            P(None, "space", "snap", None),
        ),
        check_vma=False,
    )
```
